128 devices in a mesh: row: 16 (over x, y), col: 8 (over z, core).
Axes of the slice: x: 4, y: 4, z: 4, core: 2. Of those that a mesh axis runs over, the one named last changes fastest.
Arguments:
- right_side: float32 [2, 128, 98304], P(None, None, ('row', 'col')), may hold values from -100 to 100
- self_impedance: float32 [2, 98304], P(None, ('row', 'col')), may hold values from -1 to 6, as said below
- near_blocks: bfloat16 [16, 48, 6, 2, 128, 128], P('row', 'col'), may hold values from -0.109375 to 0.109375
- near_columns: int32 [16, 48, 6], P('row', 'col'), may hold values from 0 to 47, as said below
- column_factors: bfloat16 [16, 16, 2, 64, 6144], P('row', None, None, None, 'col'), may hold values from -0.078125 to 0.078125
- row_factors: bfloat16 [16, 16, 2, 64, 6144], P('row', None, None, None, 'col'), may hold values from -0.15625 to 0.15625
- tile_ranks: int32 [16, 16], replicated, may hold values from 0 to 64, as said below
Outputs:
- solution: float32 [2, 128, 98304], P(None, None, ('row', 'col'))
- residual: float32 [2, 128, 98304], P(None, None, ('row', 'col'))
The draws below stay inside these ranges and needn't reach their ends.
Inputs may be any that keep to these rules, and one draw needn't show every extreme that they name: `self_impedance`: real parts (index 0) lie between 4 and 6, imaginary parts between -1 and 1. `near_columns`: entry [r, p, s] is a column sub-block of block r within 2 sub-blocks of row sub-block p; slot 0 holds max(p - 2, 0) and slot 1 holds min(p + 2, 47). `tile_ranks`: zero on the diagonal tiles and from 16 to 64 on all others; both 16 and 64 occur.
All inputs are finite; a program needn't handle non-finite values.
Results may differ from the reference program's by a relative error of at most 0.015.
Values may be sent and summed in bfloat16 or wider, within the bound.
No kernel may reach another device: no remote copies, remote signals or barrier semaphores. Data moves between devices by JAX's collectives and lax.ppermute only.
A program may use at most 128 MiB of HBM per device.

```python
import jax
import jax.numpy as jnp
from jax import lax

R = 128
B = 6144
K = 64
KMIN = 16
SB = 128
NNEAR = 6
HALO = 2
ITERS = 2
GRID = 16
N = 98304


def draw_right_side(key, part):
    subkeys = jax.random.split(key, 3)
    slot_position = jnp.arange(N, dtype=jnp.float32) / N
    group_level = jax.random.uniform(subkeys[1], (N // SB,), dtype=jnp.float32)
    row_scale = 3.0 ** slot_position * jnp.repeat(10.0 ** (0.5 * group_level), SB)
    column_scale = 10.0 ** jax.random.uniform(subkeys[2], (R,), dtype=jnp.float32)
    random_part = jnp.clip(jax.random.normal(subkeys[0], (2, R, N), dtype=jnp.float32), -4.0, 4.0)
    return 0.25 * column_scale[None, :, None] * row_scale[None, None, :] * random_part


def draw_self_impedance(key, part):
    subkeys = jax.random.split(key, 2)
    real_part = jax.random.uniform(subkeys[0], (N,), dtype=jnp.float32, minval=4.0, maxval=6.0)
    imag_part = jax.random.uniform(subkeys[1], (N,), dtype=jnp.float32, minval=-1.0, maxval=1.0)
    return jnp.stack([real_part, imag_part])


def draw_near_columns(key, part):
    sub_blocks = B // SB
    offsets = jax.random.randint(key, (GRID, sub_blocks, NNEAR), -HALO, HALO + 1, dtype=jnp.int32)
    offsets = offsets.at[:, :, 0].set(-HALO).at[:, :, 1].set(HALO)
    centre = jnp.arange(sub_blocks, dtype=jnp.int32)[None, :, None]
    return jnp.clip(centre + offsets, 0, sub_blocks - 1).astype(jnp.int32)


def draw_tile_ranks(key, part):
    subkeys = jax.random.split(key, 2)
    ceiling = jax.random.randint(subkeys[0], (GRID, 1), KMIN, K + 1, dtype=jnp.int32)
    rank_table = jax.random.randint(subkeys[1], (GRID, GRID), KMIN, ceiling + 1, dtype=jnp.int32)
    rank_table = rank_table.at[0, 1].set(K).at[1, 0].set(KMIN)
    diagonal = jnp.eye(GRID, dtype=jnp.int32) > 0
    return jnp.where(diagonal, 0, rank_table).astype(jnp.int32)


def levels(rng, dims, shards, least, largest):
    def one(dim, parts):
        steps = jax.random.uniform(jax.random.fold_in(jax.random.fold_in(rng, 6), dim), (parts,), jnp.float32, least / len(shards), largest / len(shards))
        return jnp.repeat(jnp.exp(steps), dims[dim] // parts).reshape((-1,) + (1,) * (len(dims) - dim - 1))

    gain = one(*shards[0])
    for cut in shards[1:]:
        gain = gain * one(*cut)
    return gain


def bell_draw(rng, shape, width, limit, shards=(), held_as=jnp.bfloat16):
    loudness = levels(rng, shape, shards, -0.22, 0.18) if shards else 1.0
    drawn = jax.random.normal(rng, shape, jnp.float32) * width * loudness
    return jnp.minimum(jnp.maximum(drawn, -limit), limit).astype(held_as)


def setup_inputs(seed: int = 0) -> dict:
    streams_of = jax.random.split(jax.random.key(seed), 8)
    right_side = draw_right_side(jax.random.fold_in(streams_of[7], 71), 0)
    self_impedance = draw_self_impedance(jax.random.fold_in(streams_of[7], 71), 0)
    near_blocks = bell_draw(streams_of[2], (GRID, B // SB, NNEAR, 2, SB, SB), (24 * SB) ** -0.5, 0.109375, ((0, 16), (1, 8)))
    near_columns = draw_near_columns(jax.random.fold_in(streams_of[7], 71), 0)
    column_factors = bell_draw(streams_of[4], (GRID, GRID, 2, K, B), B ** -0.5, 0.078125, ((0, 16), (4, 8)))
    row_factors = bell_draw(streams_of[5], (GRID, GRID, 2, K, B), (24 * K) ** -0.5, 0.15625, ((0, 16), (4, 8)))
    tile_ranks = draw_tile_ranks(jax.random.fold_in(streams_of[7], 71), 0)
    return {"right_side": right_side, "self_impedance": self_impedance, "near_blocks": near_blocks, "near_columns": near_columns, "column_factors": column_factors, "row_factors": row_factors, "tile_ranks": tile_ranks}


TOP_PRECISION = lax.Precision.HIGHEST

def complex_pair(formula, left_real, left_imag, right_real, right_imag):
    real_out = jnp.einsum(formula, left_real, right_real, precision=TOP_PRECISION) - jnp.einsum(formula, left_imag, right_imag, precision=TOP_PRECISION)
    imag_out = jnp.einsum(formula, left_real, right_imag, precision=TOP_PRECISION) + jnp.einsum(formula, left_imag, right_real, precision=TOP_PRECISION)
    return (real_out, imag_out)

def self_term(input_operand, impedance):
    real_out = impedance[0] * input_operand[0] - impedance[1] * input_operand[1]
    imag_out = impedance[0] * input_operand[1] + impedance[1] * input_operand[0]
    return jnp.stack([real_out, imag_out])

def near_product(rounded, near_blocks, near_columns):
    tiles_view = jnp.moveaxis(rounded.reshape(2, R, GRID, B // SB, SB), 2, 0)

    def one_tile(operands):
        blocks, selected_option, tile_field = operands
        picked = jnp.take(tile_field, selected_option, axis=2).astype(jnp.float32)
        weights = jnp.moveaxis(blocks, 2, 0).astype(jnp.float32)
        real_out, imag_out = complex_pair('psji,rpsj->rpi', weights[0], weights[1], picked[0], picked[1])
        return jnp.stack([real_out, imag_out]).reshape(2, R, B)
    outputs = lax.map(one_tile, (near_blocks, near_columns, tiles_view))
    return jnp.moveaxis(outputs, 0, 2).reshape(2, R, GRID * B)

def far_product(rounded, column_factors, row_factors, tile_ranks):
    tiles_view = jnp.moveaxis(rounded.reshape(2, R, GRID, B), 2, 0)

    def column_tile(operands):
        factors, tile_field = operands
        field_wide = tile_field.astype(jnp.float32)
        factors_wide = factors.astype(jnp.float32)
        real_out, imag_out = complex_pair('ikn,rn->ikr', factors_wide[:, 0], factors_wide[:, 1], field_wide[0], field_wide[1])
        return jnp.stack([real_out, imag_out], axis=1)
    products = lax.map(column_tile, (column_factors, tiles_view))
    products = jnp.swapaxes(products, 0, 1)
    rank_mask = (jnp.arange(K)[None, None, :] < tile_ranks[:, :, None]).astype(jnp.bfloat16)
    tile_coeffs = products.astype(jnp.bfloat16) * rank_mask[:, :, None, :, None]

    def row_tile(operands):
        factors, weights = operands
        factors_wide = factors.astype(jnp.float32)
        weights_wide = weights.astype(jnp.float32)
        real_out, imag_out = complex_pair('jkn,jkr->rn', factors_wide[:, 0], factors_wide[:, 1], weights_wide[:, 0], weights_wide[:, 1])
        return jnp.stack([real_out, imag_out])
    outputs = lax.map(row_tile, (row_factors, tile_coeffs))
    return jnp.moveaxis(outputs, 0, 2).reshape(2, R, GRID * B)

def inner_product(left_operand, right_operand):
    return jnp.einsum('tfg,tdg->fd', left_operand, right_operand, precision=TOP_PRECISION)

def subtract(input_operand, project_onto, basis_vectors):
    return input_operand - jnp.einsum('dp,kdf->kpf', project_onto, basis_vectors, precision=TOP_PRECISION)

def orthonormal(input_operand, gram_matrix):
    lower_triangle_factor = jnp.linalg.cholesky(gram_matrix)
    inverted_factor = jax.scipy.linalg.solve_triangular(lower_triangle_factor, jnp.eye(gram_matrix.shape[0], dtype=jnp.float32), lower=True)
    return (jnp.einsum('qf,gfl->gql', inverted_factor, input_operand, precision=TOP_PRECISION), lower_triangle_factor.T)

def least_squares(hessen_columns, first_factor, block_count):
    block_size = first_factor.shape[0]
    rows_list = []
    for slot_position in range(block_count + 1):
        pieces = []
        for column in range(block_count):
            blocks = hessen_columns[column]
            if slot_position < len(blocks):
                pieces.append(blocks[slot_position])
            else:
                pieces.append(jnp.zeros((block_size, block_size), jnp.float32))
        rows_list.append(jnp.concatenate(pieces, axis=1))
    hessenberg = jnp.concatenate(rows_list, axis=0)
    target = jnp.concatenate([first_factor, jnp.zeros((block_count * block_size, block_size), jnp.float32)], axis=0)
    normal = jnp.dot(hessenberg.T, hessenberg, precision=TOP_PRECISION)
    right_hand = jnp.dot(hessenberg.T, target, precision=TOP_PRECISION)
    coefficients = jax.scipy.linalg.cho_solve((jnp.linalg.cholesky(normal), True), right_hand)
    misfit = target - jnp.dot(hessenberg, coefficients, precision=TOP_PRECISION)
    return (coefficients, misfit)

def combine(basis_vector_list, weights):
    block_size = weights.shape[1]
    running_total = jnp.zeros(basis_vector_list[0].shape, jnp.float32)
    for slot_position in range(len(basis_vector_list)):
        selected_option = weights[slot_position * block_size:(slot_position + 1) * block_size]
        running_total = running_total + jnp.einsum('xe,uxr->uer', selected_option, basis_vector_list[slot_position], precision=TOP_PRECISION)
    return running_total

def reference(right_side, self_impedance, near_blocks, near_columns, column_factors, row_factors, tile_ranks):

    def operate(input_operand):
        rounded = input_operand.astype(jnp.bfloat16)
        result = self_term(input_operand, self_impedance)
        result = result + near_product(rounded, near_blocks, near_columns)
        return result + far_product(rounded, column_factors, row_factors, tile_ranks)
    leading, first_factor = orthonormal(right_side, inner_product(right_side, right_side))
    krylov = [leading]
    hessen_columns = []
    for iteration in range(ITERS):
        mapped = operate(krylov[iteration])
        blocks = []
        for earlier in range(iteration + 1):
            project_onto = inner_product(krylov[earlier], mapped)
            mapped = subtract(mapped, project_onto, krylov[earlier])
            blocks.append(project_onto)
        following, factor = orthonormal(mapped, inner_product(mapped, mapped))
        blocks.append(factor)
        krylov.append(following)
        hessen_columns.append(blocks)
    coefficients, misfit = least_squares(hessen_columns, first_factor, ITERS)
    solution = combine(krylov[:ITERS], coefficients)
    residual = combine(krylov, misfit)
    return (solution, residual)
```

```python
import jax
import jax.numpy as jnp
from jax import lax
from jax.sharding import Mesh, PartitionSpec as P

K = 64
SB = 128
HALO = 2
R = 128
SHIFT = 5.0

TOP = lax.Precision.HIGHEST
ALL = ("x", "y", "z", "c")


def swap(x, axis, k):
    n = lax.axis_size(axis)
    return lax.ppermute(x, axis, [(i, i ^ k) for i in range(n)])


def sum_axis(x, axis):
    one, two, three = (swap(x, axis, k) for k in (1, 2, 3))
    return (x + one) + (two + three)


def sum_all(x):
    half = x.shape[0] // 2
    core = lax.axis_index("c")
    mine = lax.dynamic_slice_in_dim(x, core * half, half, 0)
    other = lax.dynamic_slice_in_dim(x, (1 - core) * half, half, 0)
    total = mine + swap(other, "c", 1)
    for axis in ("z", "y", "x"):
        total = sum_axis(total, axis)
    other = swap(total, "c", 1)
    first = jnp.where(core == 0, total, other)
    second = jnp.where(core == 0, other, total)
    return jnp.concatenate([first, second], axis=0)


def dot(a, b):
    return jnp.dot(a, b, precision=TOP)


def inverse_factor(gram):
    lower = jnp.linalg.cholesky(gram)
    return jax.scipy.linalg.solve_triangular(lower, jnp.eye(R, dtype=jnp.float32), lower=True)


def apply_rows(matrix, block):
    return jnp.einsum("qf,gfl->gql", matrix, block, precision=TOP)


def gather_coeffs(products, rank_mask):
    parts = lax.all_to_all(products.reshape(128, 16, R), ALL, 0, 0, tiled=True)
    piece = jnp.sum(parts.reshape(16, 8, 16, R).astype(jnp.float32), axis=1).astype(jnp.bfloat16)
    core, z = lax.axis_index("c"), lax.axis_index("z")
    pieces = [piece] + [swap(piece, "z", k) for k in (1, 2, 3)]
    own = jnp.stack(pieces)
    partner = swap(own, "c", 1)
    both = jnp.stack([jnp.where(core == 0, own, partner), jnp.where(core == 0, partner, own)], axis=1)
    order = jnp.arange(4) ^ z
    chunks = jnp.take(both, order, axis=0)
    whole = jnp.transpose(chunks.reshape(8, 16, 16, R), (1, 0, 2, 3)).reshape(16, 2, K, R)
    return whole * rank_mask


def local(right_side, self_impedance, near_blocks, near_columns, column_factors, row_factors, tile_ranks):
    width = right_side.shape[2]
    sub_blocks = near_columns.shape[1]
    row_index = lax.axis_index("x") * 4 + lax.axis_index("y")
    col_index = lax.axis_index("z") * 2 + lax.axis_index("c")
    local_columns = near_columns[0] - col_index * sub_blocks + HALO
    own_ranks = lax.dynamic_index_in_dim(tile_ranks, row_index, 0, keepdims=False)
    rank_mask = (jnp.arange(K)[None, :] < own_ranks[:, None]).astype(jnp.bfloat16)[:, None, :, None]
    columns = column_factors[0].reshape(16 * 2 * K, width)
    rows = row_factors[0].reshape(16 * 2 * K, width)
    near = near_blocks[0]
    forward = [(i, i + 1) for i in range(7)]
    backward = [(i + 1, i) for i in range(7)]

    def operate(x):
        rounded = x.astype(jnp.bfloat16)
        product = lax.dot_general(
            columns, rounded.reshape(2 * R, width), (((1,), (1,)), ((), ())),
            preferred_element_type=jnp.float32,
        ).reshape(16, 2, K, 2, R)
        real = product[:, 0, :, 0] - product[:, 1, :, 1]
        imag = product[:, 0, :, 1] + product[:, 1, :, 0]
        products = jnp.stack([real, imag], axis=1).astype(jnp.bfloat16)
        low = lax.ppermute(rounded[:, :, width - HALO * SB :], ("z", "c"), forward)
        high = lax.ppermute(rounded[:, :, : HALO * SB], ("z", "c"), backward)
        widened = jnp.concatenate([low, rounded, high], axis=2).reshape(2, R, -1, SB)
        picked = jnp.take(widened, local_columns, axis=2)

        def mix(formula, left, right):
            return jnp.einsum(formula, left, right, preferred_element_type=jnp.float32)

        form = "psji,rpsj->rpi"
        near_real = mix(form, near[:, :, 0], picked[0]) - mix(form, near[:, :, 1], picked[1])
        near_imag = mix(form, near[:, :, 0], picked[1]) + mix(form, near[:, :, 1], picked[0])
        near_part = jnp.stack([near_real, near_imag]).reshape(2, R, width)
        coeffs = gather_coeffs(products, rank_mask)
        for_real = jnp.stack([coeffs[:, 0], -coeffs[:, 1]], axis=1).reshape(16 * 2 * K, R)
        for_imag = jnp.stack([coeffs[:, 1], coeffs[:, 0]], axis=1).reshape(16 * 2 * K, R)
        far_part = lax.dot_general(
            jnp.concatenate([for_real, for_imag], axis=1), rows, (((0,), (0,)), ((), ())),
            preferred_element_type=jnp.float32,
        ).reshape(2, R, width)
        real_part = self_impedance[0] - SHIFT
        imag_part = self_impedance[1]
        self_part = jnp.stack([real_part * x[0] - imag_part * x[1], real_part * x[1] + imag_part * x[0]])
        return self_part + near_part + far_part

    def inner(a, b):
        return jnp.einsum("tfg,tdg->fd", a, b, precision=TOP)

    gram = sum_all(inner(right_side, right_side))
    basis_0 = apply_rows(inverse_factor(gram), right_side)
    basis_1 = operate(basis_0)
    image_0 = basis_1 + SHIFT * basis_0
    image_1 = operate(basis_1) + SHIFT * basis_1
    b_0, b_1, a_00, a_10, a_11, _ = jnp.split(
        sum_all(
            jnp.concatenate(
                [
                    inner(image_0, right_side),
                    inner(image_1, right_side),
                    inner(image_0, image_0),
                    inner(image_1, image_0),
                    inner(image_1, image_1),
                    jnp.zeros((R, R), jnp.float32),
                ]
            )
        ),
        6,
    )
    half_0 = inverse_factor(a_00)
    cross = dot(half_0, a_10.T)
    reduced_0 = dot(half_0, b_0)
    half_1 = inverse_factor(a_11 - dot(cross.T, cross))
    y_1 = dot(half_1.T, dot(half_1, b_1 - dot(cross.T, reduced_0)))
    y_0 = dot(half_0.T, reduced_0 - dot(cross, y_1))
    solution = apply_rows(y_0.T, basis_0) + apply_rows(y_1.T, basis_1)
    residual = right_side - apply_rows(y_0.T, image_0) - apply_rows(y_1.T, image_1)
    return solution, residual


def solution(mesh):
    fine = Mesh(mesh.devices.reshape(4, 4, 4, 2), ALL)
    row, col = ("x", "y"), ("z", "c")
    placed = (
        P(None, None, ALL),
        P(None, ALL),
        P(row, col, None, None, None, None),
        P(row, col, None),
        P(row, None, None, None, col),
        P(row, None, None, None, col),
        P(),
    )
    return jax.shard_map(
        local, mesh=fine, in_specs=placed, out_specs=(P(None, None, ALL), P(None, None, ALL)), check_vma=False
    )
```

```python
import jax
import jax.numpy as jnp
from jax import lax
from jax.experimental import pallas as pl
from jax.experimental.pallas import tpu as pltpu
from jax.sharding import Mesh, PartitionSpec as P

K = 64
SB = 128
HALO = 2
R = 128
TILES = 16
SLOTS = 6
SHIFT = 5.0

TOP = lax.Precision.HIGHEST
ALL = ("x", "y", "z", "c")
VMEM = pltpu.VMEM
ANY = pl.BlockSpec(memory_space=pl.ANY)
SMEM = pl.BlockSpec(memory_space=pltpu.SMEM)
WHOLE = pl.BlockSpec(memory_space=pltpu.VMEM)
PARAMS = pltpu.CompilerParams(vmem_limit_bytes=40 * 1024 * 1024)


def dot(a, b, over=(1, 0), precision=TOP):
    dims = (((over[0],), (over[1],)), ((), ()))
    return lax.dot_general(a, b, dims, precision=precision, preferred_element_type=jnp.float32)


def bf16_dot(a, b, over=(1, 0)):
    return dot(a, b, over, None)


def inverse_factor(gram):
    lane = lax.broadcasted_iota(jnp.int32, (8, R), 1)
    sub = lax.broadcasted_iota(jnp.int32, (8, R), 0)
    one_lane = lane[:1]
    chunks = [gram[8 * j : 8 * j + 8] for j in range(R // 8)]
    floor = jnp.zeros((1, R), jnp.float32)
    for j in range(R // 8):
        floor = floor + jnp.sum(jnp.where(lane == sub + 8 * j, chunks[j], 0.0), axis=0, keepdims=True)
    floor = floor * 1e-7
    for k in range(R - 1):
        j0, i0 = divmod(k, 8)
        row = chunks[j0][i0 : i0 + 1]
        pivot = jnp.maximum(row, floor)[:, k : k + 1]
        scaled = jnp.where(one_lane == k, 1.0, row) * (1.0 / pivot)
        for j in range(j0, R // 8):
            if j == j0 and i0 == 7:
                continue
            column = chunks[j][:, k : k + 1]
            new = jnp.where(lane == k, 0.0, chunks[j]) - column * scaled
            chunks[j] = jnp.where(sub > i0, new, chunks[j]) if j == j0 else new
    for j in range(R // 8):
        diagonal = lane == sub + 8 * j
        pivots = jnp.sum(jnp.where(diagonal, jnp.maximum(chunks[j], floor), 0.0), axis=1, keepdims=True)
        unit = jnp.where(lane < sub + 8 * j, chunks[j], jnp.where(diagonal, 1.0, 0.0))
        chunks[j] = unit * lax.rsqrt(pivots)
    return jnp.concatenate(chunks, axis=0)


def send_edges(x, low_ref, high_ref):
    width = x.shape[-1]
    high_ref[...] = x[:, :, width - HALO * SB :]
    low_ref[...] = x[:, :, : HALO * SB]


def column_products(x, columns, out_ref):
    flat = x.reshape(2 * R, x.shape[2])
    sign = jnp.where(lax.broadcasted_iota(jnp.int32, (R, 2 * K), 1) < K, -1.0, 1.0)
    for i in range(TILES):
        both = bf16_dot(flat, columns[2 * K * i : 2 * K * (i + 1)], (1, 1))
        out_ref[i] = (both[:R] + sign * pltpu.roll(both[R:], K, 1)).astype(jnp.bfloat16)


def start_kernel(gram_ref, side_ref, columns_ref, basis_ref, rounded_ref, low_ref, high_ref, out_ref, columns, sem):
    copy = pltpu.make_async_copy(columns_ref, columns, sem)
    copy.start()
    factor = inverse_factor(gram_ref[...])
    for part in range(2):
        basis_ref[part] = dot(factor, side_ref[part])
    x = basis_ref[...].astype(jnp.bfloat16)
    rounded_ref[...] = x
    send_edges(x, low_ref, high_ref)
    copy.wait()
    column_products(x, columns, out_ref)


def near_kernel(where_ref, x_ref, rounded_ref, low_ref, high_ref, self_ref, near_ref, out_ref, near, wide, picked, sem):
    rows = near_ref.shape[0]
    copies = [pltpu.make_async_copy(near_ref.at[p], near.at[p], sem.at[p]) for p in range(rows)]
    for copy in copies:
        copy.start()
    width = x_ref.shape[2]
    edge = HALO * SB
    wide[:, :, :edge] = low_ref[...]
    wide[:, :, edge : edge + width] = rounded_ref[...]
    wide[:, :, edge + width :] = high_ref[...]
    real, imag = self_ref[0:1] - SHIFT, self_ref[1:2]
    for p in range(rows):
        for s in range(SLOTS):
            at = pl.multiple_of(where_ref[p, s] * SB, SB)
            picked[:R, s * SB : (s + 1) * SB] = wide[0, :, pl.ds(at, SB)]
            picked[R:, s * SB : (s + 1) * SB] = wide[1, :, pl.ds(at, SB)]
        copies[p].wait()
        by_real = bf16_dot(picked[...], near[p, :, 0].reshape(SLOTS * SB, SB))
        by_imag = bf16_dot(picked[...], near[p, :, 1].reshape(SLOTS * SB, SB))
        at = slice(p * SB, (p + 1) * SB)
        x_real, x_imag = x_ref[0, :, at], x_ref[1, :, at]
        re, im = real[:, at], imag[:, at]
        out_ref[0, :, at] = re * x_real - im * x_imag + (by_real[:R] - by_imag[R:])
        out_ref[1, :, at] = re * x_imag + im * x_real + (by_imag[:R] + by_real[R:])


def far_part(place_ref, own_ref, partner_ref, rows, tiles, left):
    z, core = place_ref[0], place_ref[1]
    for k in range(4):
        chunk = 2 * (z ^ k)
        tiles[:, pl.ds(pl.multiple_of((chunk + core) * 16, 16), 16), :] = own_ref[k]
        tiles[:, pl.ds(pl.multiple_of((chunk + 1 - core) * 16, 16), 16), :] = partner_ref[k]
    sign = jnp.where(lax.broadcasted_iota(jnp.int32, (R, 2 * K), 1) < K, 1.0, -1.0)
    for j in range(TILES):
        tile = tiles[j].astype(jnp.float32)
        at = slice(2 * K * j, 2 * K * (j + 1))
        left[:R, at] = (tile * sign).astype(jnp.bfloat16)
        left[R:, at] = pltpu.roll(tile, K, 1).astype(jnp.bfloat16)
    return bf16_dot(left[...], rows[...]).reshape(2, R, rows.shape[1])


def middle_kernel(
    place_ref, own_ref, partner_ref, base_ref, rows_ref, columns_ref,
    basis_ref, rounded_ref, low_ref, high_ref, out_ref, rows, columns, tiles, left, sem,
):
    first = pltpu.make_async_copy(rows_ref, rows, sem.at[0])
    second = pltpu.make_async_copy(columns_ref, columns, sem.at[1])
    first.start()
    second.start()
    first.wait()
    basis_ref[...] = base_ref[...] + far_part(place_ref, own_ref, partner_ref, rows, tiles, left)
    x = basis_ref[...].astype(jnp.bfloat16)
    rounded_ref[...] = x
    send_edges(x, low_ref, high_ref)
    second.wait()
    column_products(x, columns, out_ref)


def last_kernel(
    place_ref, own_ref, partner_ref, base_ref, rows_ref, side_ref, basis_0_ref, basis_1_ref,
    basis_2_ref, sums_ref, rows, tiles, left, image_0, image_1, sem,
):
    copy = pltpu.make_async_copy(rows_ref, rows, sem)
    copy.start()
    for part in range(2):
        image_0[part] = basis_1_ref[part] + SHIFT * basis_0_ref[part]
    copy.wait()
    basis_2_ref[...] = base_ref[...] + far_part(place_ref, own_ref, partner_ref, rows, tiles, left)
    for part in range(2):
        image_1[part] = basis_2_ref[part] + SHIFT * basis_1_ref[part]
    pairs = ((image_0, None), (image_1, None), (image_0, image_0), (image_1, image_0), (image_1, image_1))
    for i, (a, b) in enumerate(pairs):
        total = 0.0
        for part in range(2):
            right = side_ref[part] if b is None else b[part]
            total = total + dot(a[part], right, (1, 1))
        sums_ref[R * i : R * (i + 1)] = total


def finish_kernel(sums_ref, side_ref, basis_0_ref, basis_1_ref, basis_2_ref, solution_ref, residual_ref):
    b_0, b_1, a_00, a_10, a_11 = (sums_ref[R * i : R * (i + 1)] for i in range(5))
    half_0 = inverse_factor(a_00)
    cross = dot(half_0, a_10, (1, 1))
    reduced = dot(half_0, b_0)
    half_1 = inverse_factor(a_11 - dot(cross, cross, (0, 0)))
    tail = dot(half_1, b_1 - dot(cross, reduced, (0, 0)))
    y_1 = dot(tail, half_1, (0, 0))
    y_0 = dot(reduced - dot(cross, y_1, (1, 1)), half_0, (0, 0))
    for part in range(2):
        combined = dot(y_0, basis_0_ref[part]) + dot(y_1, basis_1_ref[part])
        solution_ref[part] = combined
        image = dot(y_0, basis_1_ref[part]) + dot(y_1, basis_2_ref[part])
        residual_ref[part] = side_ref[part] - SHIFT * combined - image


def swap(x, axis, k):
    n = lax.axis_size(axis)
    return lax.ppermute(x, axis, [(i, i ^ k) for i in range(n)])


def sum_axis(x, axis):
    one, two, three = (swap(x, axis, k) for k in (1, 2, 3))
    return (x + one) + (two + three)


def sum_all(x):
    half = x.shape[0] // 2
    core = lax.axis_index("c")
    mine = lax.dynamic_slice_in_dim(x, core * half, half, 0)
    other = lax.dynamic_slice_in_dim(x, (1 - core) * half, half, 0)
    total = mine + swap(other, "c", 1)
    for axis in ("z", "y", "x"):
        total = sum_axis(total, axis)
    other = swap(total, "c", 1)
    first = jnp.where(core == 0, total, other)
    second = jnp.where(core == 0, other, total)
    return jnp.concatenate([first, second], axis=0)


def gather_coeffs(products, mask):
    parts = lax.all_to_all(products.reshape(8 * TILES, 16, 2 * K), ALL, 0, 0, tiled=True)
    parts = parts.reshape(TILES, 8, 16, 2 * K)
    piece = jnp.sum(parts.astype(jnp.float32), axis=1).astype(jnp.bfloat16) * mask
    own = jnp.stack([piece] + [swap(piece, "z", k) for k in (1, 2, 3)])
    return own, swap(own, "c", 1)


def local(right_side, self_impedance, near_blocks, near_columns, column_factors, row_factors, tile_ranks):
    width = right_side.shape[2]
    sub_blocks = near_columns.shape[1]
    x, y, z, core = (lax.axis_index(axis) for axis in ALL)
    place = jnp.stack([z, core]).astype(jnp.int32)
    where = near_columns[0] - (2 * z + core) * sub_blocks + HALO
    ranks = lax.dynamic_index_in_dim(tile_ranks, 4 * x + y, 0, keepdims=False)
    mask = (jnp.arange(2 * K)[None, :] % K < ranks[:, None]).astype(jnp.bfloat16)[:, None, :]
    columns = column_factors[0].reshape(TILES * 2 * K, width)
    rows = row_factors[0].reshape(TILES * 2 * K, width)
    near = near_blocks[0]
    forward = [(i, i + 1) for i in range(7)]
    backward = [(i + 1, i) for i in range(7)]

    def shape(*dims, dtype=jnp.float32):
        return jax.ShapeDtypeStruct(dims, dtype)

    block = shape(2, R, width)
    rounded_block = shape(2, R, width, dtype=jnp.bfloat16)
    edge = shape(2, R, HALO * SB, dtype=jnp.bfloat16)
    products_block = shape(TILES, R, 2 * K, dtype=jnp.bfloat16)
    weights = VMEM((TILES * 2 * K, width), jnp.bfloat16)
    far_scratch = [VMEM((TILES, R, 2 * K), jnp.bfloat16), VMEM((2 * R, TILES * 2 * K), jnp.bfloat16)]

    def near_and_self(x, rounded, low, high):
        low, high = (lax.ppermute(low, ("z", "c"), backward), lax.ppermute(high, ("z", "c"), forward))
        return pl.pallas_call(
            near_kernel,
            out_shape=block,
            in_specs=[SMEM] + [WHOLE] * 5 + [ANY],
            out_specs=WHOLE,
            scratch_shapes=[
                VMEM(near.shape, jnp.bfloat16),
                VMEM((2, R, width + 2 * HALO * SB), jnp.bfloat16),
                VMEM((2 * R, SLOTS * SB), jnp.bfloat16),
                pltpu.SemaphoreType.DMA((sub_blocks,)),
            ],
            compiler_params=PARAMS,
            cost_estimate=pl.CostEstimate(flops=8 * 36 * SB**3, bytes_accessed=6 * 2**20, transcendentals=0),
        )(where, x, rounded, high, low, self_impedance, near)

    gram = sum_all(jnp.einsum("tfg,tdg->fd", right_side, right_side, precision=TOP))
    basis_0, rounded, low, high, products = pl.pallas_call(
        start_kernel,
        out_shape=(block, rounded_block, edge, edge, products_block),
        in_specs=[WHOLE, WHOLE, ANY],
        out_specs=(WHOLE,) * 5,
        scratch_shapes=[weights, pltpu.SemaphoreType.DMA],
        compiler_params=PARAMS,
    )(gram, right_side, columns)
    own, partner = gather_coeffs(products, mask)
    base = near_and_self(basis_0, rounded, low, high)
    basis_1, rounded, low, high, products = pl.pallas_call(
        middle_kernel,
        out_shape=(block, rounded_block, edge, edge, products_block),
        in_specs=[SMEM] + [WHOLE] * 3 + [ANY] * 2,
        out_specs=(WHOLE,) * 5,
        scratch_shapes=[weights, weights, *far_scratch, pltpu.SemaphoreType.DMA((2,))],
        compiler_params=PARAMS,
    )(place, own, partner, base, rows, columns)
    own, partner = gather_coeffs(products, mask)
    base = near_and_self(basis_1, rounded, low, high)
    image = VMEM((2, R, width), jnp.float32)
    basis_2, sums = pl.pallas_call(
        last_kernel,
        out_shape=(block, shape(5 * R, R)),
        in_specs=[SMEM] + [WHOLE] * 3 + [ANY] + [WHOLE] * 3,
        out_specs=(WHOLE,) * 2,
        scratch_shapes=[weights, *far_scratch, image, image, pltpu.SemaphoreType.DMA],
        compiler_params=PARAMS,
    )(place, own, partner, base, rows, right_side, basis_0, basis_1)
    return pl.pallas_call(
        finish_kernel,
        out_shape=(block, block),
        in_specs=[WHOLE] * 5,
        out_specs=(WHOLE,) * 2,
        compiler_params=PARAMS,
    )(sum_all(sums), right_side, basis_0, basis_1, basis_2)


def solution(mesh):
    fine = Mesh(mesh.devices.reshape(4, 4, 4, 2), ALL)
    row, col = ("x", "y"), ("z", "c")
    placed = (
        P(None, None, ALL),
        P(None, ALL),
        P(row, col, None, None, None, None),
        P(row, col, None),
        P(row, None, None, None, col),
        P(row, None, None, None, col),
        P(),
    )
    return jax.shard_map(
        local, mesh=fine, in_specs=placed, out_specs=(P(None, None, ALL), P(None, None, ALL)), check_vma=False
    )
```

```python
import jax
import jax.numpy as jnp
from jax import lax
from jax.experimental import pallas as pl
from jax.experimental.pallas import tpu as pltpu
from jax.sharding import Mesh, PartitionSpec as P


K = 64
SB = 128
HALO = 2
R = 128
TILES = 16
SLOTS = 6
SHIFT = 5.0

TOP = lax.Precision.HIGHEST
ALL = ("x", "y", "z", "c")
VMEM = pltpu.VMEM
SMEM = pl.BlockSpec(memory_space=pltpu.SMEM)
WHOLE = pl.BlockSpec(memory_space=pltpu.VMEM)
PARAMS = pltpu.CompilerParams(vmem_limit_bytes=12 * 1024 * 1024)


def dot(a, b, over=(1, 0), precision=TOP):
    dims = (((over[0],), (over[1],)), ((), ()))
    return lax.dot_general(a, b, dims, precision=precision, preferred_element_type=jnp.float32)


def bf16_dot(a, b, over=(1, 0)):
    return dot(a, b, over, None)


def inverse_factor(gram):
    lane = lax.broadcasted_iota(jnp.int32, (8, R), 1)
    sub = lax.broadcasted_iota(jnp.int32, (8, R), 0)
    chunks = [gram[8 * j : 8 * j + 8] for j in range(R // 8)]
    floor = jnp.zeros((1, R), jnp.float32)
    for j in range(R // 8):
        floor = floor + jnp.sum(jnp.where(lane == sub + 8 * j, chunks[j], 0.0), axis=0, keepdims=True)
    floor = floor * 1e-7

    def full(x):
        return jnp.broadcast_to(x, (8, R))

    finished = []
    for j in range(R // 8):
        start = 8 * j
        inside = (lane >= start) & (lane < start + 8)
        rows = [full(chunks[j][t : t + 1]) for t in range(8)]
        pivots = [[full(rows[t][:, start + u : start + u + 1]) for u in range(8)] for t in range(8)]
        least = [full(floor[:, start + t : start + t + 1]) for t in range(8)]
        rows = [jnp.where(inside, jnp.where(lane == start + t, 1.0, 0.0), rows[t]) for t in range(8)]
        inverse = [None] * 8
        unit = [[None] * 8 for _ in range(8)]
        for t in range(8):
            pivots[t][t] = jnp.maximum(pivots[t][t], least[t])
            inverse[t] = 1.0 / pivots[t][t]
            for u in range(t + 1, 8):
                factor = pivots[t][u] * inverse[t]
                rows[u] = rows[u] - factor * rows[t]
                for s in range(t):
                    unit[u][s] = unit[u][s] - factor * unit[t][s]
                unit[u][t] = -factor
                for v in range(u, 8):
                    pivots[u][v] = pivots[u][v] - factor * pivots[t][v]
        done = jnp.zeros((8, R), jnp.float32)
        for t in range(8):
            done = jnp.where(sub == t, rows[t] * lax.rsqrt(pivots[t][t]), done)
        finished.append(jnp.where(lane <= sub + start, done, 0.0))
        solved = []
        for t in range(8):
            total = rows[t] * inverse[t]
            for u in range(t + 1, 8):
                total = total + (unit[u][t] * inverse[u]) * rows[u]
            solved.append(total)
        for i in range(j + 1, R // 8):
            chunk = chunks[i]
            terms = [chunk[:, start + t : start + t + 1] * solved[t] for t in range(8)]
            while len(terms) > 1:
                terms = [p + q for p, q in zip(terms[::2], terms[1::2])]
            chunks[i] = jnp.where(inside, 0.0, chunk) - terms[0]
    return jnp.concatenate(finished, axis=0)


def send_edges(x, low_ref, high_ref):
    width = x.shape[-1]
    high_ref[...] = x[:, :, width - HALO * SB :]
    low_ref[...] = x[:, :, : HALO * SB]


def column_products(x, columns, out_ref):
    flat = x.reshape(2 * R, x.shape[2])
    sign = jnp.where(lax.broadcasted_iota(jnp.int32, (R, 2 * K), 1) < K, -1.0, 1.0)
    for i in range(TILES):
        both = bf16_dot(flat, columns[2 * K * i : 2 * K * (i + 1)], (1, 1))
        out_ref[i] = (both[:R] + sign * pltpu.roll(both[R:], K, 1)).astype(jnp.bfloat16)


def gram_kernel(place_ref, side_ref, out_ref, whole):
    whole[...] = dot(side_ref[0], side_ref[0], (1, 1)) + dot(side_ref[1], side_ref[1], (1, 1))
    core = place_ref[1]
    for d in range(2):
        out_ref[d] = whole[pl.ds(pl.multiple_of((core ^ d) * (R // 2), R // 2), R // 2)]


def start_kernel(
    place_ref, mine_ref, other_ref, side_ref, columns_ref, basis_ref, rounded_ref, low_ref, high_ref, out_ref, gram
):
    core = place_ref[1]
    gram[pl.ds(pl.multiple_of(core * (R // 2), R // 2), R // 2)] = mine_ref[...]
    gram[pl.ds(pl.multiple_of((1 - core) * (R // 2), R // 2), R // 2)] = other_ref[...]
    factor = inverse_factor(gram[...])
    for part in range(2):
        basis_ref[part] = dot(factor, side_ref[part])
    x = basis_ref[...].astype(jnp.bfloat16)
    rounded_ref[...] = x
    send_edges(x, low_ref, high_ref)
    column_products(x, columns_ref, out_ref)


def near_kernel(where_ref, x_ref, rounded_ref, low_ref, high_ref, self_ref, near_ref, out_ref, wide, picked):
    width = x_ref.shape[2]
    edge = HALO * SB
    wide[:, :, :edge] = low_ref[...]
    wide[:, :, edge : edge + width] = rounded_ref[...]
    wide[:, :, edge + width :] = high_ref[...]
    real, imag = self_ref[0:1] - SHIFT, self_ref[1:2]
    for p in range(near_ref.shape[0]):
        for s in range(SLOTS):
            at = pl.multiple_of(where_ref[p, s] * SB, SB)
            picked[p % 2, :R, s * SB : (s + 1) * SB] = wide[0, :, pl.ds(at, SB)]
            picked[p % 2, R:, s * SB : (s + 1) * SB] = wide[1, :, pl.ds(at, SB)]
        by_real = bf16_dot(picked[p % 2], near_ref[p, :, 0].reshape(SLOTS * SB, SB))
        by_imag = bf16_dot(picked[p % 2], near_ref[p, :, 1].reshape(SLOTS * SB, SB))
        at = slice(p * SB, (p + 1) * SB)
        x_real, x_imag = x_ref[0, :, at], x_ref[1, :, at]
        re, im = real[:, at], imag[:, at]
        out_ref[0, :, at] = re * x_real - im * x_imag + (by_real[:R] - by_imag[R:])
        out_ref[1, :, at] = re * x_imag + im * x_real + (by_imag[:R] + by_real[R:])


def far_part(place_ref, ranks_ref, own_ref, partner_ref, rows_ref, tiles, left):
    z, core = place_ref[0], place_ref[1]
    for k in range(4):
        chunk = 2 * (z ^ k)
        tiles[:, pl.ds(pl.multiple_of((chunk + core) * 16, 16), 16), :] = own_ref[k]
        tiles[:, pl.ds(pl.multiple_of((chunk + 1 - core) * 16, 16), 16), :] = partner_ref[k]
    lane = lax.broadcasted_iota(jnp.int32, (R, 2 * K), 1)
    rank = jnp.where(lane < K, lane, lane - K)
    sign = jnp.where(lane < K, 1.0, -1.0)
    for j in range(TILES):
        tile = jnp.where(rank < ranks_ref[j], tiles[j].astype(jnp.float32), 0.0)
        at = slice(2 * K * j, 2 * K * (j + 1))
        left[:R, at] = (tile * sign).astype(jnp.bfloat16)
        left[R:, at] = pltpu.roll(tile, K, 1).astype(jnp.bfloat16)
    return bf16_dot(left[...], rows_ref[...]).reshape(2, R, rows_ref.shape[1])


def middle_kernel(
    place_ref, ranks_ref, own_ref, partner_ref, base_ref, rows_ref, columns_ref,
    basis_ref, rounded_ref, low_ref, high_ref, out_ref, tiles, left,
):
    basis_ref[...] = base_ref[...] + far_part(place_ref, ranks_ref, own_ref, partner_ref, rows_ref, tiles, left)
    x = basis_ref[...].astype(jnp.bfloat16)
    rounded_ref[...] = x
    send_edges(x, low_ref, high_ref)
    column_products(x, columns_ref, out_ref)


def last_kernel(
    place_ref, ranks_ref, own_ref, partner_ref, base_ref, rows_ref, side_ref, basis_0_ref, basis_1_ref,
    basis_2_ref, sums_ref, tiles, left, image_0, image_1, sums,
):
    image_0[...] = basis_1_ref[...] + SHIFT * basis_0_ref[...]
    basis_2_ref[...] = base_ref[...] + far_part(place_ref, ranks_ref, own_ref, partner_ref, rows_ref, tiles, left)
    image_1[...] = basis_2_ref[...] + SHIFT * basis_1_ref[...]
    pairs = (
        (image_0, side_ref), (image_1, side_ref), (image_0, image_0), (image_1, image_0), (image_1, image_1),
    )
    for i, (a, b) in enumerate(pairs):
        sums[R * i : R * (i + 1)] = dot(a[0], b[0], (1, 1)) + dot(a[1], b[1], (1, 1))
    z, core = place_ref[0], place_ref[1]
    size = sums_ref.shape[2]
    for d in range(2):
        for k in range(4):
            sums_ref[d, k] = sums[pl.ds(pl.multiple_of((4 * (core ^ d) + (z ^ k)) * size, 8), size)]


def finish_kernel(
    place_ref, own_ref, partner_ref, side_ref, basis_0_ref, basis_1_ref, basis_2_ref, solution_ref, residual_ref, sums
):
    z, core = place_ref[0], place_ref[1]
    size = own_ref.shape[1]
    for d, ref in enumerate((own_ref, partner_ref)):
        for k in range(4):
            sums[pl.ds(pl.multiple_of((4 * (core ^ d) + (z ^ k)) * size, 8), size)] = ref[k]
    b_0, b_1, a_00, a_10, a_11 = (sums[R * i : R * (i + 1)] for i in range(5))
    half_0 = inverse_factor(a_00)
    cross = dot(half_0, a_10, (1, 1))
    reduced = dot(half_0, b_0)
    half_1 = inverse_factor(a_11 - dot(cross, cross, (0, 0)))
    tail = dot(half_1, b_1 - dot(cross, reduced, (0, 0)))
    y_1 = dot(tail, half_1, (0, 0))
    y_0 = dot(reduced - dot(cross, y_1, (1, 1)), half_0, (0, 0))
    for part in range(2):
        combined = dot(y_0, basis_0_ref[part]) + dot(y_1, basis_1_ref[part])
        solution_ref[part] = combined
        image = dot(y_0, basis_1_ref[part]) + dot(y_1, basis_2_ref[part])
        residual_ref[part] = side_ref[part] - SHIFT * combined - image


def swap(x, axis, k):
    n = lax.axis_size(axis)
    return lax.ppermute(x, axis, [(i, i ^ k) for i in range(n)])


def sum_axis(x, axis):
    one, two, three = (swap(x, axis, k) for k in (1, 2, 3))
    return (x + one) + (two + three)


def sum_halves(x):
    total = x[0] + swap(x[1], "c", 1)
    for axis in ("z", "y", "x"):
        total = sum_axis(total, axis)
    return total, swap(total, "c", 1)


def gather_z(piece):
    own = jnp.stack([piece] + [swap(piece, "z", k) for k in (1, 2, 3)])
    return own, swap(own, "c", 1)


def sum_pieces(x):
    pair = x[0] + swap(x[1], "c", 1)
    one, two, three = (swap(pair[k], "z", k) for k in (1, 2, 3))
    total = (pair[0] + one) + (two + three)
    for axis in ("y", "x"):
        total = sum_axis(total, axis)
    return gather_z(total)


def gather_coeffs(products):
    parts = lax.all_to_all(products.reshape(8 * TILES, 16, 2 * K), ALL, 0, 0, tiled=True)
    parts = parts.reshape(TILES, 8, 16, 2 * K)
    return gather_z(jnp.sum(parts.astype(jnp.float32), axis=1).astype(jnp.bfloat16))


def local(right_side, self_impedance, near_blocks, near_columns, column_factors, row_factors, tile_ranks):
    width = right_side.shape[2]
    sub_blocks = near_columns.shape[1]
    x, y, z, core = (lax.axis_index(axis) for axis in ALL)
    place = jnp.stack([z, core]).astype(jnp.int32)
    where = near_columns[0] - (2 * z + core) * sub_blocks + HALO
    ranks = lax.dynamic_index_in_dim(tile_ranks, 4 * x + y, 0, keepdims=False)
    columns = column_factors[0].reshape(TILES * 2 * K, width)
    rows = row_factors[0].reshape(TILES * 2 * K, width)
    near = near_blocks[0]
    forward = [(i, i + 1) for i in range(7)]
    backward = [(i + 1, i) for i in range(7)]

    def shape(*dims, dtype=jnp.float32):
        return jax.ShapeDtypeStruct(dims, dtype)

    block = shape(2, R, width)
    rounded_block = shape(2, R, width, dtype=jnp.bfloat16)
    edge = shape(2, R, HALO * SB, dtype=jnp.bfloat16)
    products_block = shape(TILES, R, 2 * K, dtype=jnp.bfloat16)
    far_scratch = [VMEM((TILES, R, 2 * K), jnp.bfloat16), VMEM((2 * R, TILES * 2 * K), jnp.bfloat16)]

    def call(kernel, out_shape, smem, scratch, *args, flops=10**8):
        many = isinstance(out_shape, tuple)
        return pl.pallas_call(
            kernel,
            out_shape=out_shape,
            in_specs=[SMEM] * smem + [WHOLE] * (len(args) - smem),
            out_specs=(WHOLE,) * len(out_shape) if many else WHOLE,
            scratch_shapes=scratch,
            compiler_params=PARAMS,
            cost_estimate=pl.CostEstimate(flops=flops, bytes_accessed=6 * 2**20, transcendentals=0),
        )(*args)

    def operate(x, rounded, low, high, products):
        from_right = lax.ppermute(low, ("z", "c"), backward)
        from_left = lax.ppermute(high, ("z", "c"), forward)
        own, partner = gather_coeffs(products)
        base = call(
            near_kernel,
            block,
            1,
            [
                VMEM((2, R, width + 2 * HALO * SB), jnp.bfloat16),
                VMEM((2, 2 * R, SLOTS * SB), jnp.bfloat16),
            ],
            where, x, rounded, from_left, from_right, self_impedance, near,
            flops=8 * 36 * SB**3,
        )
        return own, partner, base

    half = shape(2, R // 2, R)
    gram = call(gram_kernel, half, 1, [VMEM((R, R), jnp.float32)], place, right_side)
    basis_0, *rest = call(
        start_kernel, (block, rounded_block, edge, edge, products_block), 1, [VMEM((R, R), jnp.float32)],
        place, *sum_halves(gram), right_side, columns,
    )
    applied = operate(basis_0, *rest)
    basis_1, *rest = call(
        middle_kernel, (block, rounded_block, edge, edge, products_block), 2, far_scratch,
        place, ranks, *applied, rows, columns,
    )
    applied = operate(basis_1, *rest)
    image = VMEM((2, R, width), jnp.float32)
    basis_2, sums = call(
        last_kernel, (block, shape(2, 4, 5 * R // 8, R)), 2,
        [*far_scratch, image, image, VMEM((5 * R, R), jnp.float32)],
        place, ranks, *applied, rows, right_side, basis_0, basis_1,
    )
    return call(
        finish_kernel, (block, block), 1, [VMEM((5 * R, R), jnp.float32)],
        place, *sum_pieces(sums), right_side, basis_0, basis_1, basis_2,
    )


def solution(mesh):
    fine = Mesh(mesh.devices.reshape(4, 4, 4, 2), ALL)
    row, col = ("x", "y"), ("z", "c")
    placed = (
        P(None, None, ALL),
        P(None, ALL),
        P(row, col, None, None, None, None),
        P(row, col, None),
        P(row, None, None, None, col),
        P(row, None, None, None, col),
        P(),
    )
    return jax.shard_map(
        local, mesh=fine, in_specs=placed, out_specs=(P(None, None, ALL), P(None, None, ALL)), check_vma=False
    )
```

```python
import jax
import jax.numpy as jnp
from jax import lax
from jax.experimental import pallas as pl
from jax.experimental.pallas import tpu as pltpu
from jax.sharding import Mesh, PartitionSpec as P


K = 64
SB = 128
HALO = 2
R = 128
TILES = 16
SLOTS = 6
SHIFT = 5.0

TOP = lax.Precision.HIGHEST
ALL = ("x", "y", "z", "c")
VMEM = pltpu.VMEM
SMEM = pl.BlockSpec(memory_space=pltpu.SMEM)
ANY = pl.BlockSpec(memory_space=pl.ANY)
WHOLE = pl.BlockSpec(memory_space=pltpu.VMEM)
SMALL, LARGE = 12 * 2**20, 60 * 1024 * 1024


def dot(a, b, over=(1, 0), precision=TOP):
    dims = (((over[0],), (over[1],)), ((), ()))
    return lax.dot_general(a, b, dims, precision=precision, preferred_element_type=jnp.float32)


def bf16_dot(a, b, over=(1, 0)):
    return dot(a, b, over, None)


def inverse_factor(gram):
    lane = lax.broadcasted_iota(jnp.int32, (8, R), 1)
    sub = lax.broadcasted_iota(jnp.int32, (8, R), 0)
    chunks = [gram[8 * j : 8 * j + 8] for j in range(R // 8)]
    floor = jnp.zeros((1, R), jnp.float32)
    for j in range(R // 8):
        floor = floor + jnp.sum(jnp.where(lane == sub + 8 * j, chunks[j], 0.0), axis=0, keepdims=True)
    floor = floor * 1e-7

    def full(x):
        return jnp.broadcast_to(x, (8, R))

    finished = []
    for j in range(R // 8):
        start = 8 * j
        inside = (lane >= start) & (lane < start + 8)
        rows = [full(chunks[j][t : t + 1]) for t in range(8)]
        pivots = [[full(rows[t][:, start + u : start + u + 1]) for u in range(8)] for t in range(8)]
        least = [full(floor[:, start + t : start + t + 1]) for t in range(8)]
        rows = [jnp.where(inside, jnp.where(lane == start + t, 1.0, 0.0), rows[t]) for t in range(8)]
        inverse = [None] * 8
        unit = [[None] * 8 for _ in range(8)]
        for t in range(8):
            pivots[t][t] = jnp.maximum(pivots[t][t], least[t])
            inverse[t] = 1.0 / pivots[t][t]
            for u in range(t + 1, 8):
                factor = pivots[t][u] * inverse[t]
                rows[u] = rows[u] - factor * rows[t]
                for s in range(t):
                    unit[u][s] = unit[u][s] - factor * unit[t][s]
                unit[u][t] = -factor
                for v in range(u, 8):
                    pivots[u][v] = pivots[u][v] - factor * pivots[t][v]
        done = jnp.zeros((8, R), jnp.float32)
        for t in range(8):
            done = jnp.where(sub == t, rows[t] * lax.rsqrt(pivots[t][t]), done)
        finished.append(jnp.where(lane <= sub + start, done, 0.0))
        solved = []
        for t in range(8):
            total = rows[t] * inverse[t]
            for u in range(t + 1, 8):
                total = total + (unit[u][t] * inverse[u]) * rows[u]
            solved.append(total)
        for i in range(j + 1, R // 8):
            chunk = chunks[i]
            terms = [chunk[:, start + t : start + t + 1] * solved[t] for t in range(8)]
            while len(terms) > 1:
                terms = [p + q for p, q in zip(terms[::2], terms[1::2])]
            chunks[i] = jnp.where(inside, 0.0, chunk) - terms[0]
    return jnp.concatenate(finished, axis=0)


class Copies:
    def __init__(self, sems):
        self.sems, self.count = sems, 0

    def start(self, source, target):
        copy = pltpu.make_async_copy(source, target, self.sems.at[self.count])
        self.count += 1
        copy.start()
        return copy


def wait(copies):
    for copy in copies:
        copy.wait()


def aligned(index, size):
    return pl.ds(pl.multiple_of(index * size, size), size)


def column_products(copies, x, columns, out, out_ref):
    flat = x.reshape(2 * R, x.shape[2])
    sign = jnp.where(lax.broadcasted_iota(jnp.int32, (R, 2 * K), 1) < K, -1.0, 1.0)
    sent = []
    for i in range(TILES):
        both = bf16_dot(flat, columns[2 * K * i : 2 * K * (i + 1)], (1, 1))
        out[i] = (both[:R] + sign * pltpu.roll(both[R:], K, 1)).astype(jnp.bfloat16)
        if i % 4 == 3:
            sent.append(copies.start(out.at[i - 3 : i + 1], out_ref.at[i - 3 : i + 1]))
    return sent


def send_basis(copies, basis, rounded, basis_ref, rounded_ref, low_ref, high_ref):
    width = basis.shape[2]
    return [
        copies.start(rounded.at[:, :, : HALO * SB], low_ref),
        copies.start(rounded.at[:, :, width - HALO * SB :], high_ref),
        copies.start(rounded, rounded_ref),
        copies.start(basis, basis_ref),
    ]


def gram_kernel(place_ref, side_ref, out_ref, whole):
    whole[...] = dot(side_ref[0], side_ref[0], (1, 1)) + dot(side_ref[1], side_ref[1], (1, 1))
    core = place_ref[1]
    for d in range(2):
        out_ref[d] = whole[aligned(core ^ d, R // 2)]


def start_kernel(
    place_ref, mine_ref, other_ref, side_ref, columns_ref, basis_ref, rounded_ref, low_ref, high_ref, out_ref,
    gram, side, columns, basis, rounded, out, sems,
):
    copies = Copies(sems)
    core = place_ref[1]
    side_copy = copies.start(side_ref, side)
    columns_copy = copies.start(columns_ref, columns)
    gram[aligned(core, R // 2)] = mine_ref[...]
    gram[aligned(1 - core, R // 2)] = other_ref[...]
    factor = inverse_factor(gram[...])
    side_copy.wait()
    for part in range(2):
        basis[part] = dot(factor, side[part])
    x = basis[...].astype(jnp.bfloat16)
    rounded[...] = x
    sent = send_basis(copies, basis, rounded, basis_ref, rounded_ref, low_ref, high_ref)
    columns_copy.wait()
    sent += column_products(copies, x, columns, out, out_ref)
    wait(sent)


def near_kernel(
    where_ref, x_ref, rounded_ref, low_ref, high_ref, self_ref, near_ref, out_ref,
    x, wide, impedance, near, picked, out, sems,
):
    copies = Copies(sems)
    width = x.shape[2]
    edge = HALO * SB
    first = [
        copies.start(low_ref, wide.at[:, :, :edge]),
        copies.start(rounded_ref, wide.at[:, :, edge : edge + width]),
        copies.start(high_ref, wide.at[:, :, edge + width :]),
        copies.start(self_ref, impedance),
    ]
    second = [copies.start(near_ref, near), copies.start(x_ref, x)]
    wait(first)
    impedance[0:1] = impedance[0:1] - SHIFT
    wait(second)

    def one(p, carry):
        for s in range(SLOTS):
            at = aligned(where_ref[p, s], SB)
            picked[:R, s * SB : (s + 1) * SB] = wide[0, :, at]
            picked[R:, s * SB : (s + 1) * SB] = wide[1, :, at]
        by_real = bf16_dot(picked[...], near[p, :, 0].reshape(SLOTS * SB, SB))
        by_imag = bf16_dot(picked[...], near[p, :, 1].reshape(SLOTS * SB, SB))
        at = aligned(p, SB)
        x_real, x_imag = x[0, :, at], x[1, :, at]
        re, im = impedance[0:1, at], impedance[1:2, at]
        out[0, :, at] = re * x_real - im * x_imag + (by_real[:R] - by_imag[R:])
        out[1, :, at] = re * x_imag + im * x_real + (by_imag[:R] + by_real[R:])
        return carry

    lax.fori_loop(0, near.shape[0], one, 0)
    copies.start(out, out_ref).wait()


def place_tiles(place_ref, own_ref, partner_ref, tiles):
    z, core = place_ref[0], place_ref[1]
    for k in range(4):
        chunk = 2 * (z ^ k)
        tiles[:, aligned(chunk + core, 16)] = own_ref[k]
        tiles[:, aligned(chunk + 1 - core, 16)] = partner_ref[k]


def far_part(place_ref, ranks_ref, own_ref, partner_ref, rows, tiles, left):
    place_tiles(place_ref, own_ref, partner_ref, tiles)
    lane = lax.broadcasted_iota(jnp.int32, (R, 2 * K), 1)
    rank = jnp.where(lane < K, lane, lane - K)
    sign = jnp.where(lane < K, 1.0, -1.0)
    for j in range(TILES):
        tile = jnp.where(rank < ranks_ref[j], tiles[j].astype(jnp.float32), 0.0)
        at = slice(2 * K * j, 2 * K * (j + 1))
        left[:R, at] = (tile * sign).astype(jnp.bfloat16)
        left[R:, at] = pltpu.roll(tile, K, 1).astype(jnp.bfloat16)
    return bf16_dot(left[...], rows[...]).reshape(2, R, rows.shape[1])


def middle_kernel(
    place_ref, ranks_ref, own_ref, partner_ref, rows, base_ref, columns_ref,
    basis_ref, rounded_ref, low_ref, high_ref, out_ref,
    tiles, left, columns, basis, rounded, out, sems,
):
    copies = Copies(sems)
    base_copy = copies.start(base_ref, basis)
    columns_copy = copies.start(columns_ref, columns)
    far = far_part(place_ref, ranks_ref, own_ref, partner_ref, rows, tiles, left)
    base_copy.wait()
    basis[...] = basis[...] + far
    x = basis[...].astype(jnp.bfloat16)
    rounded[...] = x
    sent = send_basis(copies, basis, rounded, basis_ref, rounded_ref, low_ref, high_ref)
    columns_copy.wait()
    sent += column_products(copies, x, columns, out, out_ref)
    wait(sent)


def last_kernel(
    place_ref, ranks_ref, own_ref, partner_ref, rows, base_ref, side_ref, basis_0_ref, basis_1_ref,
    basis_2_ref, sums_ref, tiles, left, basis, images, sums, sems,
):
    copies = Copies(sems)
    others = [copies.start(ref, basis.at[i]) for i, ref in enumerate((basis_0_ref, basis_1_ref, base_ref))]
    others += [copies.start(side_ref.at[part], images.at[part, :R]) for part in range(2)]
    far = far_part(place_ref, ranks_ref, own_ref, partner_ref, rows, tiles, left)
    wait(others)
    basis[2] = basis[2] + far
    sent = [copies.start(basis.at[2], basis_2_ref)]
    for j in range(2):
        for part in range(2):
            images[part, R * (j + 1) : R * (j + 2)] = basis[j + 1, part] + SHIFT * basis[j, part]
    total = [dot(images[part, R:], images[part, : 2 * R], (1, 1)) for part in range(2)]
    total = total[0] + total[1]
    last = [dot(images[part, 2 * R :], images[part, 2 * R :], (1, 1)) for part in range(2)]
    sums[: 2 * R] = total[:, :R]
    sums[2 * R : 4 * R] = total[:, R:]
    sums[4 * R :] = last[0] + last[1]
    z, core = place_ref[0], place_ref[1]
    size = sums_ref.shape[2]
    for d in range(2):
        for k in range(4):
            sums_ref[d, k] = sums[aligned(4 * (core ^ d) + (z ^ k), size)]
    wait(sent)


def finish_kernel(
    place_ref, own_ref, partner_ref, side_ref, basis_0_ref, basis_1_ref, basis_2_ref, solution_ref, residual_ref,
    sums, halves, work, cross, basis, side, solved, left_over, sems,
):
    copies = Copies(sems)
    z, core = place_ref[0], place_ref[1]
    size = own_ref.shape[1]
    for d, ref in enumerate((own_ref, partner_ref)):
        for k in range(4):
            sums[aligned(4 * (core ^ d) + (z ^ k), size)] = ref[k]
    others = [copies.start(side_ref, side)]
    for i, ref in enumerate((basis_0_ref, basis_1_ref, basis_2_ref)):
        others += [copies.start(ref.at[part], basis.at[part, R * i : R * (i + 1)]) for part in range(2)]
    b_0, b_1, a_00, a_10, a_11 = (sums.at[R * i : R * (i + 1)] for i in range(5))
    work[...] = a_00[...]

    def factor(i, carry):
        halves[i] = inverse_factor(work[...])

        @pl.when(i == 0)
        def _():
            cross[...] = dot(halves[0], a_10[...], (1, 1))
            work[...] = a_11[...] - dot(cross[...], cross[...], (0, 0))

        return carry

    lax.fori_loop(0, 2, factor, 0)
    reduced = dot(halves[0], b_0[...])
    tail = dot(halves[1], b_1[...] - dot(cross[...], reduced, (0, 0)))
    y_1 = dot(tail, halves[1], (0, 0))
    y_0 = dot(reduced - dot(cross[...], y_1, (1, 1)), halves[0], (0, 0))
    weights = jnp.concatenate([y_0, y_1], axis=1)
    wait(others)
    sent = []
    for part in range(2):
        solved[part] = dot(weights, basis[part, : 2 * R])
        sent.append(copies.start(solved.at[part], solution_ref.at[part]))
        left_over[part] = side[part] - SHIFT * solved[part] - dot(weights, basis[part, R:])
        sent.append(copies.start(left_over.at[part], residual_ref.at[part]))
    wait(sent)


def swap(x, axis, k):
    n = lax.axis_size(axis)
    return lax.ppermute(x, axis, [(i, i ^ k) for i in range(n)])


def sum_axis(x, axis):
    one, two, three = (swap(x, axis, k) for k in (1, 2, 3))
    return (x + one) + (two + three)


def sum_halves(x):
    total = x[0] + swap(x[1], "c", 1)
    for axis in ("z", "y", "x"):
        total = sum_axis(total, axis)
    return total, swap(total, "c", 1)


def gather_z(piece):
    own = jnp.stack([piece] + [swap(piece, "z", k) for k in (1, 2, 3)])
    return own, swap(own, "c", 1)


def sum_pieces(x):
    pair = x[0] + swap(x[1], "c", 1)
    one, two, three = (swap(pair[k], "z", k) for k in (1, 2, 3))
    total = (pair[0] + one) + (two + three)
    for axis in ("y", "x"):
        total = sum_axis(total, axis)
    return gather_z(total)


def gather_coeffs(products):
    parts = lax.all_to_all(products.reshape(8 * TILES, 16, 2 * K), ALL, 0, 0, tiled=True)
    parts = parts.reshape(TILES, 8, 16, 2 * K)
    return gather_z(jnp.sum(parts.astype(jnp.float32), axis=1).astype(jnp.bfloat16))


def local(right_side, self_impedance, near_blocks, near_columns, column_factors, row_factors, tile_ranks):
    width = right_side.shape[2]
    sub_blocks = near_columns.shape[1]
    x, y, z, core = (lax.axis_index(axis) for axis in ALL)
    place = jnp.stack([z, core]).astype(jnp.int32)
    where = near_columns[0] - (2 * z + core) * sub_blocks + HALO
    ranks = lax.dynamic_index_in_dim(tile_ranks, 4 * x + y, 0, keepdims=False)
    columns = column_factors[0].reshape(TILES * 2 * K, width)
    rows = row_factors[0].reshape(TILES * 2 * K, width)
    near = near_blocks[0]
    forward = [(i, i + 1) for i in range(7)]
    backward = [(i + 1, i) for i in range(7)]

    def shape(*dims, dtype=jnp.float32):
        return jax.ShapeDtypeStruct(dims, dtype)

    block = shape(2, R, width)
    rounded_block = shape(2, R, width, dtype=jnp.bfloat16)
    edge = shape(2, R, HALO * SB, dtype=jnp.bfloat16)
    products_block = shape(TILES, R, 2 * K, dtype=jnp.bfloat16)
    wide = VMEM((2, R, width), jnp.float32)
    rounded_scratch = VMEM((2, R, width), jnp.bfloat16)
    products_scratch = VMEM((TILES, R, 2 * K), jnp.bfloat16)
    weights = VMEM((TILES * 2 * K, width), jnp.bfloat16)
    far_scratch = [products_scratch, VMEM((2 * R, TILES * 2 * K), jnp.bfloat16)]
    square = VMEM((R, R), jnp.float32)
    outer = VMEM((5 * R, R), jnp.float32)
    stacked = VMEM((2, 3 * R, width), jnp.float32)

    def call(kernel, out_specs, smem, vmem, scratch, copies, *args, limit=LARGE):
        if copies:
            scratch = [*scratch, pltpu.SemaphoreType.DMA((copies,))]
        return pl.pallas_call(
            kernel,
            out_shape=tuple(kind for kind, _ in out_specs),
            in_specs=[SMEM] * smem + [WHOLE] * vmem + [ANY] * (len(args) - smem - vmem),
            out_specs=tuple(space for _, space in out_specs),
            scratch_shapes=scratch,
            compiler_params=pltpu.CompilerParams(vmem_limit_bytes=limit),
            cost_estimate=pl.CostEstimate(flops=3 * 10**8, bytes_accessed=6 * 2**20, transcendentals=0),
        )(*args)

    def operate(x, rounded, low, high, products):
        from_right = lax.ppermute(low, ("z", "c"), backward)
        from_left = lax.ppermute(high, ("z", "c"), forward)
        own, partner = gather_coeffs(products)
        (base,) = call(
            near_kernel,
            ((block, ANY),),
            1,
            0,
            [
                wide,
                VMEM((2, R, width + 2 * HALO * SB), jnp.bfloat16),
                VMEM((2, width), jnp.float32),
                VMEM(near.shape, jnp.bfloat16),
                VMEM((2 * R, SLOTS * SB), jnp.bfloat16),
                wide,
            ],
            7,
            where, x, rounded, from_left, from_right, self_impedance, near,
        )
        return own, partner, base

    (gram,) = call(
        gram_kernel, ((shape(2, R // 2, R), WHOLE),), 1, 1, [square], 0, place, right_side, limit=SMALL
    )
    operands = ((block, ANY), (rounded_block, ANY), (edge, ANY), (edge, ANY), (products_block, ANY))
    basis_0, *rest = call(
        start_kernel, operands, 1, 2, [square, wide, weights, wide, rounded_scratch, products_scratch], 10,
        place, *sum_halves(gram), right_side, columns,
    )
    own, partner, base = operate(basis_0, *rest)
    basis_1, *rest = call(
        middle_kernel, operands, 2, 3, [*far_scratch, weights, wide, rounded_scratch, products_scratch], 10,
        place, ranks, own, partner, rows, base, columns,
    )
    own, partner, base = operate(basis_1, *rest)
    basis_2, sums = call(
        last_kernel, ((block, ANY), (shape(2, 4, 5 * R // 8, R), WHOLE)), 2, 3,
        [*far_scratch, VMEM((3, 2, R, width), jnp.float32), stacked, outer], 6,
        place, ranks, own, partner, rows, base, right_side, basis_0, basis_1,
    )
    return call(
        finish_kernel, ((block, ANY), (block, ANY)), 1, 2,
        [outer, VMEM((2, R, R), jnp.float32), square, square, stacked, wide, wide, wide], 11,
        place, *sum_pieces(sums), right_side, basis_0, basis_1, basis_2,
    )


def solution(mesh):
    fine = Mesh(mesh.devices.reshape(4, 4, 4, 2), ALL)
    row, col = ("x", "y"), ("z", "c")
    placed = (
        P(None, None, ALL),
        P(None, ALL),
        P(row, col, None, None, None, None),
        P(row, col, None),
        P(row, None, None, None, col),
        P(row, None, None, None, col),
        P(),
    )
    return jax.shard_map(
        local, mesh=fine, in_specs=placed, out_specs=(P(None, None, ALL), P(None, None, ALL)), check_vma=False
    )
```

```python
import jax
import jax.numpy as jnp
from jax import lax
from jax.experimental import pallas as pl
from jax.experimental.pallas import tpu as pltpu
from jax.sharding import Mesh, PartitionSpec as P


K = 64
SB = 128
HALO = 2
R = 128
TILES = 16
SLOTS = 6
SHIFT = 5.0

TOP = lax.Precision.HIGHEST
ALL = ("x", "y", "z", "c")
VMEM = pltpu.VMEM
SMEM = pl.BlockSpec(memory_space=pltpu.SMEM)
ANY = pl.BlockSpec(memory_space=pl.ANY)
WHOLE = pl.BlockSpec(memory_space=pltpu.VMEM)
SMALL, LARGE = 12 * 2**20, 60 * 2**20


def dot(a, b, over=(1, 0), precision=TOP):
    dims = (((over[0],), (over[1],)), ((), ()))
    return lax.dot_general(a, b, dims, precision=precision, preferred_element_type=jnp.float32)


def bf16_dot(a, b, over=(1, 0)):
    return dot(a, b, over, None)


def inverse_factor(gram):
    lane = lax.broadcasted_iota(jnp.int32, (8, R), 1)
    sub = lax.broadcasted_iota(jnp.int32, (8, R), 0)
    chunks = [gram[8 * j : 8 * j + 8] for j in range(R // 8)]
    floor = jnp.zeros((1, R), jnp.float32)
    for j in range(R // 8):
        floor = floor + jnp.sum(jnp.where(lane == sub + 8 * j, chunks[j], 0.0), axis=0, keepdims=True)
    floor = floor * 1e-7

    def full(x):
        return jnp.broadcast_to(x, (8, R))

    finished = []
    for j in range(R // 8):
        start = 8 * j
        inside = (lane >= start) & (lane < start + 8)
        rows = [full(chunks[j][t : t + 1]) for t in range(8)]
        pivots = [[full(rows[t][:, start + u : start + u + 1]) for u in range(8)] for t in range(8)]
        least = [full(floor[:, start + t : start + t + 1]) for t in range(8)]
        rows = [jnp.where(inside, jnp.where(lane == start + t, 1.0, 0.0), rows[t]) for t in range(8)]
        inverse = [None] * 8
        unit = [[None] * 8 for _ in range(8)]

        def eliminate(u, t, factor):
            rows[u] = rows[u] - factor * rows[t]
            for s in range(t):
                unit[u][s] = unit[u][s] - factor * unit[t][s] if s in known[u] else -factor * unit[t][s]
                known[u].add(s)
            unit[u][t] = -factor
            known[u].add(t)

        known = [set() for _ in range(8)]
        for t in range(0, 8, 2):
            n = t + 1
            first = jnp.maximum(pivots[t][t], least[t])
            off, second = pivots[t][n], pivots[n][n]
            area = jnp.maximum(first * second - off * off, first * least[n])
            by_first, by_area = 1.0 / first, 1.0 / area
            pivots[t][t], inverse[t] = first, by_first
            pivots[n][n], inverse[n] = area * by_first, first * by_area
            ratio = off * by_first
            left = {u: (second * pivots[t][u] - off * pivots[n][u]) * by_area for u in range(t + 2, 8)}
            right = {u: (first * pivots[n][u] - off * pivots[t][u]) * by_area for u in range(t + 2, 8)}
            plain = {u: pivots[t][u] * by_first for u in range(t + 2, 8)}
            for u in range(t + 2, 8):
                for v in range(u, 8):
                    pivots[u][v] = pivots[u][v] - (left[u] * pivots[t][v] + right[u] * pivots[n][v])
            eliminate(n, t, ratio)
            for u in range(t + 2, 8):
                eliminate(u, t, plain[u])
                eliminate(u, n, right[u])
        done = jnp.zeros((8, R), jnp.float32)
        for t in range(8):
            done = jnp.where(sub == t, rows[t] * lax.rsqrt(pivots[t][t]), done)
        finished.append(jnp.where(lane <= sub + start, done, 0.0))
        solved = []
        for t in range(8):
            total = rows[t] * inverse[t]
            for u in range(t + 1, 8):
                total = total + (unit[u][t] * inverse[u]) * rows[u]
            solved.append(total)
        for i in range(j + 1, R // 8):
            chunk = chunks[i]
            terms = [chunk[:, start + t : start + t + 1] * solved[t] for t in range(8)]
            while len(terms) > 1:
                terms = [p + q for p, q in zip(terms[::2], terms[1::2])]
            chunks[i] = jnp.where(inside, 0.0, chunk) - terms[0]
    return jnp.concatenate(finished, axis=0)


class Copies:
    def __init__(self, sems):
        self.sems, self.count = sems, 0

    def start(self, source, target):
        copy = pltpu.make_async_copy(source, target, self.sems.at[self.count])
        self.count += 1
        copy.start()
        return copy


def wait(copies):
    for copy in copies:
        copy.wait()


def aligned(index, size):
    return pl.ds(pl.multiple_of(index * size, size), size)


def column_products(copies, x, columns, out, out_ref):
    flat = x.reshape(2 * R, x.shape[2])
    sign = jnp.where(lax.broadcasted_iota(jnp.int32, (R, 2 * K), 1) < K, -1.0, 1.0)
    sent = []
    for i in range(0, TILES, 2):
        both = bf16_dot(flat, columns[2 * K * i : 2 * K * (i + 2)], (1, 1))
        for j in range(2):
            top, bottom = (both[R * h : R * (h + 1), R * j : R * (j + 1)] for h in range(2))
            out[i + j] = (top + sign * pltpu.roll(bottom, K, 1)).astype(jnp.bfloat16)
        if i % 4 == 2:
            sent.append(copies.start(out.at[i - 2 : i + 2], out_ref.at[i - 2 : i + 2]))
    return sent


def send_basis(copies, basis, rounded, basis_ref, rounded_ref, low_ref, high_ref):
    width = basis.shape[2]
    return [
        copies.start(rounded.at[:, :, : HALO * SB], low_ref),
        copies.start(rounded.at[:, :, width - HALO * SB :], high_ref),
        copies.start(rounded, rounded_ref),
        copies.start(basis, basis_ref),
    ]


def gram_kernel(place_ref, side_ref, mine_ref, other_ref, whole):
    whole[...] = dot(side_ref[0], side_ref[0], (1, 1)) + dot(side_ref[1], side_ref[1], (1, 1))
    core = place_ref[1]
    for d, ref in enumerate((mine_ref, other_ref)):
        ref[...] = whole[aligned(core ^ d, R // 2)]


def start_kernel(
    place_ref, mine_ref, other_ref, side_ref, columns_ref, basis_ref, rounded_ref, low_ref, high_ref, out_ref,
    gram, side, columns, basis, rounded, out, sems,
):
    copies = Copies(sems)
    core = place_ref[1]
    side_copy = copies.start(side_ref, side)
    columns_copy = copies.start(columns_ref, columns)
    gram[aligned(core, R // 2)] = mine_ref[...]
    gram[aligned(1 - core, R // 2)] = other_ref[...]
    factor = inverse_factor(gram[...])
    side_copy.wait()
    for part in range(2):
        basis[part] = dot(factor, side[part])
    x = basis[...].astype(jnp.bfloat16)
    rounded[...] = x
    sent = send_basis(copies, basis, rounded, basis_ref, rounded_ref, low_ref, high_ref)
    columns_copy.wait()
    sent += column_products(copies, x, columns, out, out_ref)
    wait(sent)


def near_kernel(
    where_ref, x_ref, rounded_ref, low_ref, high_ref, self_ref, near_ref, out_ref,
    x, wide, impedance, near, picked, out, sems,
):
    copies = Copies(sems)
    width = x.shape[2]
    edge = HALO * SB
    first = [
        copies.start(low_ref, wide.at[:, :, :edge]),
        copies.start(rounded_ref, wide.at[:, :, edge : edge + width]),
        copies.start(high_ref, wide.at[:, :, edge + width :]),
        copies.start(self_ref, impedance),
    ]
    second = [copies.start(near_ref, near), copies.start(x_ref, x)]
    wait(first)
    impedance[0:1] = impedance[0:1] - SHIFT
    wait(second)

    def one(p, carry):
        for s in range(SLOTS):
            at = aligned(where_ref[p, s], SB)
            picked[:R, s * SB : (s + 1) * SB] = wide[0, :, at]
            picked[R:, s * SB : (s + 1) * SB] = wide[1, :, at]
        by_real = bf16_dot(picked[...], near[p, :, 0].reshape(SLOTS * SB, SB))
        by_imag = bf16_dot(picked[...], near[p, :, 1].reshape(SLOTS * SB, SB))
        at = aligned(p, SB)
        x_real, x_imag = x[0, :, at], x[1, :, at]
        re, im = impedance[0:1, at], impedance[1:2, at]
        out[0, :, at] = re * x_real - im * x_imag + (by_real[:R] - by_imag[R:])
        out[1, :, at] = re * x_imag + im * x_real + (by_imag[:R] + by_real[R:])
        return carry

    lax.fori_loop(0, near.shape[0], one, 0)
    copies.start(out, out_ref).wait()


def place_tiles(place_ref, own_ref, partner_ref, tiles):
    z, core = place_ref[0], place_ref[1]
    for k in range(4):
        chunk = 2 * (z ^ k)
        tiles[:, aligned(chunk + core, 16)] = own_ref[k]
        tiles[:, aligned(chunk + 1 - core, 16)] = partner_ref[k]


def far_part(place_ref, ranks_ref, own_ref, partner_ref, rows_copy, rows, tiles, left):
    place_tiles(place_ref, own_ref, partner_ref, tiles)
    lane = lax.broadcasted_iota(jnp.int32, (R, 2 * K), 1)
    rank = jnp.where(lane < K, lane, lane - K)
    sign = jnp.where(lane < K, 1.0, -1.0)
    for j in range(TILES):
        tile = jnp.where(rank < ranks_ref[place_ref[2], j], tiles[j].astype(jnp.float32), 0.0)
        at = slice(2 * K * j, 2 * K * (j + 1))
        left[:R, at] = (tile * sign).astype(jnp.bfloat16)
        left[R:, at] = pltpu.roll(tile, K, 1).astype(jnp.bfloat16)
    rows_copy.wait()
    return bf16_dot(left[...], rows[...]).reshape(2, R, rows.shape[1])


def middle_kernel(
    place_ref, ranks_ref, own_ref, partner_ref, rows_ref, base_ref, columns_ref,
    basis_ref, rounded_ref, low_ref, high_ref, out_ref,
    tiles, left, rows, columns, basis, rounded, out, sems,
):
    copies = Copies(sems)
    rows_copy = copies.start(rows_ref, rows)
    base_copy = copies.start(base_ref, basis)
    columns_copy = copies.start(columns_ref, columns)
    far = far_part(place_ref, ranks_ref, own_ref, partner_ref, rows_copy, rows, tiles, left)
    base_copy.wait()
    basis[...] = basis[...] + far
    x = basis[...].astype(jnp.bfloat16)
    rounded[...] = x
    sent = send_basis(copies, basis, rounded, basis_ref, rounded_ref, low_ref, high_ref)
    columns_copy.wait()
    sent += column_products(copies, x, columns, out, out_ref)
    wait(sent)


def last_kernel(
    place_ref, ranks_ref, own_ref, partner_ref, rows_ref, base_ref, side_ref, basis_0_ref, basis_1_ref,
    basis_2_ref, mine_ref, other_ref, tiles, left, rows, basis, images, sums, sems,
):
    copies = Copies(sems)
    rows_copy = copies.start(rows_ref, rows)
    others = [copies.start(ref, basis.at[i]) for i, ref in enumerate((basis_0_ref, basis_1_ref, base_ref))]
    others += [copies.start(side_ref.at[part], images.at[part, :R]) for part in range(2)]
    far = far_part(place_ref, ranks_ref, own_ref, partner_ref, rows_copy, rows, tiles, left)
    wait(others)
    basis[2] = basis[2] + far
    sent = [copies.start(basis.at[2], basis_2_ref)]
    for j in range(2):
        for part in range(2):
            images[part, R * (j + 1) : R * (j + 2)] = basis[j + 1, part] + SHIFT * basis[j, part]
    total = [dot(images[part, R:], images[part, : 2 * R], (1, 1)) for part in range(2)]
    total = total[0] + total[1]
    last = [dot(images[part, 2 * R :], images[part, 2 * R :], (1, 1)) for part in range(2)]
    sums[: 2 * R] = total[:, :R]
    sums[2 * R : 4 * R] = total[:, R:]
    sums[4 * R :] = last[0] + last[1]
    z, core = place_ref[0], place_ref[1]
    size = mine_ref.shape[1]
    for d, ref in enumerate((mine_ref, other_ref)):
        for k in range(4):
            ref[k] = sums[aligned(4 * (core ^ d) + (z ^ k), size)]
    wait(sent)


def finish_kernel(
    place_ref, own_ref, partner_ref, side_ref, basis_0_ref, basis_1_ref, basis_2_ref, solution_ref, residual_ref,
    sums, halves, work, cross, basis, side, solved, left_over, sems,
):
    copies = Copies(sems)
    z, core = place_ref[0], place_ref[1]
    size = own_ref.shape[1]
    for d, ref in enumerate((own_ref, partner_ref)):
        for k in range(4):
            sums[aligned(4 * (core ^ d) + (z ^ k), size)] = ref[k]
    others = [copies.start(side_ref, side)]
    for i, ref in enumerate((basis_0_ref, basis_1_ref, basis_2_ref)):
        others += [copies.start(ref.at[part], basis.at[part, R * i : R * (i + 1)]) for part in range(2)]
    b_0, b_1, a_00, a_10, a_11 = (sums.at[R * i : R * (i + 1)] for i in range(5))
    work[...] = a_00[...]

    def factor(i, carry):
        halves[i] = inverse_factor(work[...])

        @pl.when(i == 0)
        def _():
            cross[...] = dot(halves[0], a_10[...], (1, 1))
            work[...] = a_11[...] - dot(cross[...], cross[...], (0, 0))

        return carry

    lax.fori_loop(0, 2, factor, 0)
    reduced = dot(halves[0], b_0[...])
    tail = dot(halves[1], b_1[...] - dot(cross[...], reduced, (0, 0)))
    y_1 = dot(tail, halves[1], (0, 0))
    y_0 = dot(reduced - dot(cross[...], y_1, (1, 1)), halves[0], (0, 0))
    weights = jnp.concatenate([y_0, y_1], axis=1)
    wait(others)
    sent = []
    for part in range(2):
        solved[part] = dot(weights, basis[part, : 2 * R])
        sent.append(copies.start(solved.at[part], solution_ref.at[part]))
        left_over[part] = side[part] - SHIFT * solved[part] - dot(weights, basis[part, R:])
        sent.append(copies.start(left_over.at[part], residual_ref.at[part]))
    wait(sent)


def swap(x, axis, k):
    n = lax.axis_size(axis)
    return lax.ppermute(x, axis, [(i, i ^ k) for i in range(n)])


def sum_axis(x, axis):
    one, two, three = (swap(x, axis, k) for k in (1, 2, 3))
    return (x + one) + (two + three)


def sum_halves(mine, other):
    total = mine + swap(other, "c", 1)
    for axis in ("z", "y", "x"):
        total = sum_axis(total, axis)
    return total, swap(total, "c", 1)


def gather_z(piece):
    own = jnp.stack([piece] + [swap(piece, "z", k) for k in (1, 2, 3)])
    return own, swap(own, "c", 1)


def sum_pieces(mine, other):
    pair = mine + swap(other, "c", 1)
    one, two, three = (swap(pair[k], "z", k) for k in (1, 2, 3))
    total = (pair[0] + one) + (two + three)
    for axis in ("y", "x"):
        total = sum_axis(total, axis)
    return gather_z(total)


def gather_coeffs(products):
    parts = lax.all_to_all(products.reshape(8 * TILES, 16, 2 * K), ALL, 0, 0, tiled=True)
    parts = parts.reshape(TILES, 8, 16, 2 * K)
    return gather_z(jnp.sum(parts.astype(jnp.float32), axis=1).astype(jnp.bfloat16))


def local(right_side, self_impedance, near_blocks, near_columns, column_factors, row_factors, tile_ranks):
    width = right_side.shape[2]
    sub_blocks = near_columns.shape[1]
    x, y, z, core = (lax.axis_index(axis) for axis in ALL)
    place = jnp.stack([z, core, 4 * x + y]).astype(jnp.int32)
    where = near_columns[0] - (2 * z + core) * sub_blocks + HALO
    columns = column_factors[0].reshape(TILES * 2 * K, width)
    rows = row_factors[0].reshape(TILES * 2 * K, width)
    near = near_blocks[0]
    forward = [(i, i + 1) for i in range(7)]
    backward = [(i + 1, i) for i in range(7)]

    def shape(*dims, dtype=jnp.float32):
        return jax.ShapeDtypeStruct(dims, dtype)

    block = shape(2, R, width)
    rounded_block = shape(2, R, width, dtype=jnp.bfloat16)
    edge = shape(2, R, HALO * SB, dtype=jnp.bfloat16)
    products_block = shape(TILES, R, 2 * K, dtype=jnp.bfloat16)
    wide = VMEM((2, R, width), jnp.float32)
    rounded_scratch = VMEM((2, R, width), jnp.bfloat16)
    products_scratch = VMEM((TILES, R, 2 * K), jnp.bfloat16)
    weights = VMEM((TILES * 2 * K, width), jnp.bfloat16)
    far_scratch = [products_scratch, VMEM((2 * R, TILES * 2 * K), jnp.bfloat16), weights]
    square = VMEM((R, R), jnp.float32)
    outer = VMEM((5 * R, R), jnp.float32)
    stacked = VMEM((2, 3 * R, width), jnp.float32)

    def call(kernel, out_specs, smem, vmem, scratch, copies, *args, limit=LARGE):
        if copies:
            scratch = [*scratch, pltpu.SemaphoreType.DMA((copies,))]
        return pl.pallas_call(
            kernel,
            out_shape=tuple(kind for kind, _ in out_specs),
            in_specs=[SMEM] * smem + [WHOLE] * vmem + [ANY] * (len(args) - smem - vmem),
            out_specs=tuple(space for _, space in out_specs),
            scratch_shapes=scratch,
            compiler_params=pltpu.CompilerParams(vmem_limit_bytes=limit),
            cost_estimate=pl.CostEstimate(flops=3 * 10**8, bytes_accessed=6 * 2**20, transcendentals=0),
        )(*args)

    def operate(x, rounded, low, high, products):
        from_right = lax.ppermute(low, ("z", "c"), backward)
        from_left = lax.ppermute(high, ("z", "c"), forward)
        own, partner = gather_coeffs(products)
        (base,) = call(
            near_kernel,
            ((block, ANY),),
            1,
            0,
            [
                wide,
                VMEM((2, R, width + 2 * HALO * SB), jnp.bfloat16),
                VMEM((2, width), jnp.float32),
                VMEM(near.shape, jnp.bfloat16),
                VMEM((2 * R, SLOTS * SB), jnp.bfloat16),
                wide,
            ],
            7,
            where, x, rounded, from_left, from_right, self_impedance, near,
        )
        return own, partner, base

    half = (shape(R // 2, R), WHOLE)
    gram = call(gram_kernel, (half, half), 1, 1, [square], 0, place, right_side, limit=SMALL)
    operands = ((block, ANY), (rounded_block, ANY), (edge, ANY), (edge, ANY), (products_block, ANY))
    basis_0, *rest = call(
        start_kernel, operands, 1, 2, [square, wide, weights, wide, rounded_scratch, products_scratch], 10,
        place, *sum_halves(*gram), right_side, columns,
    )
    own, partner, base = operate(basis_0, *rest)
    basis_1, *rest = call(
        middle_kernel, operands, 2, 2, [*far_scratch, weights, wide, rounded_scratch, products_scratch], 11,
        place, tile_ranks, own, partner, rows, base, columns,
    )
    own, partner, base = operate(basis_1, *rest)
    pieces = (shape(4, 5 * R // 8, R), WHOLE)
    basis_2, *sums = call(
        last_kernel, ((block, ANY), pieces, pieces), 2, 2,
        [*far_scratch, VMEM((3, 2, R, width), jnp.float32), stacked, outer], 7,
        place, tile_ranks, own, partner, rows, base, right_side, basis_0, basis_1,
    )
    return call(
        finish_kernel, ((block, ANY), (block, ANY)), 1, 2,
        [outer, VMEM((2, R, R), jnp.float32), square, square, stacked, wide, wide, wide], 11,
        place, *sum_pieces(*sums), right_side, basis_0, basis_1, basis_2,
    )


def solution(mesh):
    fine = Mesh(mesh.devices.reshape(4, 4, 4, 2), ALL)
    row, col = ("x", "y"), ("z", "c")
    placed = (
        P(None, None, ALL),
        P(None, ALL),
        P(row, col, None, None, None, None),
        P(row, col, None),
        P(row, None, None, None, col),
        P(row, None, None, None, col),
        P(),
    )
    return jax.shard_map(
        local, mesh=fine, in_specs=placed, out_specs=(P(None, None, ALL), P(None, None, ALL)), check_vma=False
    )
```

```python
import jax
import jax.numpy as jnp
from jax import lax
from jax.experimental import pallas as pl
from jax.experimental.pallas import tpu as pltpu
from jax.sharding import Mesh, PartitionSpec as P


K = 64
SB = 128
HALO = 2
R = 128
TILES = 16
SLOTS = 6
SHIFT = 5.0

TOP = lax.Precision.HIGHEST
ALL = ("x", "y", "z", "c")
VMEM = pltpu.VMEM
SMEM = pl.BlockSpec(memory_space=pltpu.SMEM)
ANY = pl.BlockSpec(memory_space=pl.ANY)
WHOLE = pl.BlockSpec(memory_space=pltpu.VMEM)
SMALL, LARGE = 12 * 2**20, 60 * 2**20


def dot(a, b, over=(1, 0), precision=TOP):
    dims = (((over[0],), (over[1],)), ((), ()))
    return lax.dot_general(a, b, dims, precision=precision, preferred_element_type=jnp.float32)


def bf16_dot(a, b, over=(1, 0)):
    return dot(a, b, over, None)


def inverse_factor(gram):
    lane = lax.broadcasted_iota(jnp.int32, (8, R), 1)
    sub = lax.broadcasted_iota(jnp.int32, (8, R), 0)
    chunks = [gram[8 * j : 8 * j + 8] for j in range(R // 8)]
    floor = jnp.zeros((1, R), jnp.float32)
    for j in range(R // 8):
        floor = floor + jnp.sum(jnp.where(lane == sub + 8 * j, chunks[j], 0.0), axis=0, keepdims=True)
    floor = floor * 1e-7

    def full(x):
        return jnp.broadcast_to(x, (8, R))

    finished = []
    for j in range(R // 8):
        start = 8 * j
        inside = (lane >= start) & (lane < start + 8)
        rows = [full(chunks[j][t : t + 1]) for t in range(8)]
        pivots = [[full(rows[t][:, start + u : start + u + 1]) for u in range(8)] for t in range(8)]
        least = [full(floor[:, start + t : start + t + 1]) for t in range(8)]
        rows = [jnp.where(inside, jnp.where(lane == start + t, 1.0, 0.0), rows[t]) for t in range(8)]
        inverse = [None] * 8
        unit = [[None] * 8 for _ in range(8)]

        def eliminate(u, t, factor):
            rows[u] = rows[u] - factor * rows[t]
            for s in range(t):
                unit[u][s] = unit[u][s] - factor * unit[t][s] if s in known[u] else -factor * unit[t][s]
                known[u].add(s)
            unit[u][t] = -factor
            known[u].add(t)

        known = [set() for _ in range(8)]
        for t in range(0, 8, 2):
            n = t + 1
            first = jnp.maximum(pivots[t][t], least[t])
            off, second = pivots[t][n], pivots[n][n]
            area = jnp.maximum(first * second - off * off, first * least[n])
            by_first, by_area = 1.0 / first, 1.0 / area
            pivots[t][t], inverse[t] = first, by_first
            pivots[n][n], inverse[n] = area * by_first, first * by_area
            ratio = off * by_first
            left = {u: (second * pivots[t][u] - off * pivots[n][u]) * by_area for u in range(t + 2, 8)}
            right = {u: (first * pivots[n][u] - off * pivots[t][u]) * by_area for u in range(t + 2, 8)}
            plain = {u: pivots[t][u] * by_first for u in range(t + 2, 8)}
            for u in range(t + 2, 8):
                for v in range(u, 8):
                    pivots[u][v] = pivots[u][v] - (left[u] * pivots[t][v] + right[u] * pivots[n][v])
            eliminate(n, t, ratio)
            for u in range(t + 2, 8):
                eliminate(u, t, plain[u])
                eliminate(u, n, right[u])
        done = jnp.zeros((8, R), jnp.float32)
        for t in range(8):
            done = jnp.where(sub == t, rows[t] * lax.rsqrt(pivots[t][t]), done)
        finished.append(jnp.where(lane <= sub + start, done, 0.0))
        solved = []
        for t in range(8):
            total = rows[t] * inverse[t]
            for u in range(t + 1, 8):
                total = total + (unit[u][t] * inverse[u]) * rows[u]
            solved.append(total)
        for i in range(j + 1, R // 8):
            chunk = chunks[i]
            terms = [chunk[:, start + t : start + t + 1] * solved[t] for t in range(8)]
            while len(terms) > 1:
                terms = [p + q for p, q in zip(terms[::2], terms[1::2])]
            chunks[i] = jnp.where(inside, 0.0, chunk) - terms[0]
    return jnp.concatenate(finished, axis=0)


class Copies:
    def __init__(self, sems):
        self.sems, self.count = sems, 0

    def start(self, source, target):
        copy = pltpu.make_async_copy(source, target, self.sems.at[self.count])
        self.count += 1
        copy.start()
        return copy


def wait(copies):
    for copy in copies:
        copy.wait()


def aligned(index, size):
    return pl.ds(pl.multiple_of(index * size, size), size)


def column_products(copies, x, columns, out, out_ref):
    flat = x.reshape(2 * R, x.shape[2])
    sign = jnp.where(lax.broadcasted_iota(jnp.int32, (R, 2 * K), 1) < K, -1.0, 1.0)
    sent = []
    for i in range(0, TILES, 2):
        both = bf16_dot(flat, columns[2 * K * i : 2 * K * (i + 2)], (1, 1))
        for j in range(2):
            top, bottom = (both[R * h : R * (h + 1), R * j : R * (j + 1)] for h in range(2))
            out[i + j] = (top + sign * pltpu.roll(bottom, K, 1)).astype(jnp.bfloat16)
        if i % 4 == 2:
            sent.append(copies.start(out.at[i - 2 : i + 2], out_ref.at[i - 2 : i + 2]))
    return sent


def send_basis(copies, basis, rounded, basis_ref, rounded_ref, low_ref, high_ref):
    width = basis.shape[2]
    return [
        copies.start(rounded.at[:, :, : HALO * SB], low_ref),
        copies.start(rounded.at[:, :, width - HALO * SB :], high_ref),
        copies.start(rounded, rounded_ref),
        copies.start(basis, basis_ref),
    ]


def gram_kernel(place_ref, side_ref, mine_ref, other_ref, whole):
    whole[...] = dot(side_ref[0], side_ref[0], (1, 1)) + dot(side_ref[1], side_ref[1], (1, 1))
    core = place_ref[1]
    for d, ref in enumerate((mine_ref, other_ref)):
        ref[...] = whole[aligned(core ^ d, R // 2)]


def start_kernel(
    place_ref, mine_ref, other_ref, side_ref, columns_ref, basis_ref, rounded_ref, low_ref, high_ref, out_ref,
    gram, side, columns, basis, rounded, out, sems,
):
    copies = Copies(sems)
    core = place_ref[1]
    side_copy = copies.start(side_ref, side)
    columns_copy = copies.start(columns_ref, columns)
    gram[aligned(core, R // 2)] = mine_ref[...]
    gram[aligned(1 - core, R // 2)] = other_ref[...]
    factor = inverse_factor(gram[...])
    side_copy.wait()
    for part in range(2):
        basis[part] = dot(factor, side[part])
    x = basis[...].astype(jnp.bfloat16)
    rounded[...] = x
    sent = send_basis(copies, basis, rounded, basis_ref, rounded_ref, low_ref, high_ref)
    columns_copy.wait()
    sent += column_products(copies, x, columns, out, out_ref)
    wait(sent)


def near_kernel(
    where_ref, x_ref, rounded_ref, low_ref, high_ref, self_ref, near_ref, out_ref,
    x, wide, impedance, near, picked, out, sems,
):
    copies = Copies(sems)
    width = x.shape[2]
    edge = HALO * SB
    first = [
        copies.start(low_ref, wide.at[:, :, :edge]),
        copies.start(rounded_ref, wide.at[:, :, edge : edge + width]),
        copies.start(high_ref, wide.at[:, :, edge + width :]),
        copies.start(self_ref, impedance),
    ]
    second = [copies.start(near_ref, near), copies.start(x_ref, x)]
    wait(first)
    impedance[0:1] = impedance[0:1] - SHIFT
    wait(second)

    def one(p, carry):
        for s in range(SLOTS):
            at = aligned(where_ref[p, s], SB)
            picked[:R, s * SB : (s + 1) * SB] = wide[0, :, at]
            picked[R:, s * SB : (s + 1) * SB] = wide[1, :, at]
        pair = [near[p, :, part].reshape(SLOTS * SB, SB) for part in range(2)]
        both = bf16_dot(picked[...], jnp.concatenate(pair, axis=1))
        by_real, by_imag = both[:, :SB], both[:, SB:]
        at = aligned(p, SB)
        x_real, x_imag = x[0, :, at], x[1, :, at]
        re, im = impedance[0:1, at], impedance[1:2, at]
        out[0, :, at] = re * x_real - im * x_imag + (by_real[:R] - by_imag[R:])
        out[1, :, at] = re * x_imag + im * x_real + (by_imag[:R] + by_real[R:])
        return carry

    lax.fori_loop(0, near.shape[0], one, 0)
    copies.start(out, out_ref).wait()


def place_tiles(place_ref, own_ref, partner_ref, tiles):
    z, core = place_ref[0], place_ref[1]
    for k in range(4):
        chunk = 2 * (z ^ k)
        tiles[:, aligned(chunk + core, 16)] = own_ref[k]
        tiles[:, aligned(chunk + 1 - core, 16)] = partner_ref[k]


def far_part(place_ref, ranks_ref, own_ref, partner_ref, rows_copy, rows, tiles, left):
    place_tiles(place_ref, own_ref, partner_ref, tiles)
    lane = lax.broadcasted_iota(jnp.int32, (R, 2 * K), 1)
    rank = jnp.where(lane < K, lane, lane - K)
    sign = jnp.where(lane < K, 1.0, -1.0)
    for j in range(TILES):
        tile = jnp.where(rank < ranks_ref[place_ref[2], j], tiles[j].astype(jnp.float32), 0.0)
        at = slice(2 * K * j, 2 * K * (j + 1))
        left[:R, at] = (tile * sign).astype(jnp.bfloat16)
        left[R:, at] = pltpu.roll(tile, K, 1).astype(jnp.bfloat16)
    rows_copy.wait()
    return bf16_dot(left[...], rows[...]).reshape(2, R, rows.shape[1])


def middle_kernel(
    place_ref, ranks_ref, own_ref, partner_ref, rows_ref, base_ref, columns_ref,
    basis_ref, rounded_ref, low_ref, high_ref, out_ref,
    tiles, left, rows, columns, basis, rounded, out, sems,
):
    copies = Copies(sems)
    rows_copy = copies.start(rows_ref, rows)
    base_copy = copies.start(base_ref, basis)
    columns_copy = copies.start(columns_ref, columns)
    far = far_part(place_ref, ranks_ref, own_ref, partner_ref, rows_copy, rows, tiles, left)
    base_copy.wait()
    basis[...] = basis[...] + far
    x = basis[...].astype(jnp.bfloat16)
    rounded[...] = x
    sent = send_basis(copies, basis, rounded, basis_ref, rounded_ref, low_ref, high_ref)
    columns_copy.wait()
    sent += column_products(copies, x, columns, out, out_ref)
    wait(sent)


def last_kernel(
    place_ref, ranks_ref, own_ref, partner_ref, rows_ref, base_ref, side_ref, basis_0_ref, basis_1_ref,
    basis_2_ref, mine_ref, other_ref, tiles, left, rows, basis, images, sums, sems,
):
    copies = Copies(sems)
    rows_copy = copies.start(rows_ref, rows)
    others = [copies.start(ref, basis.at[i]) for i, ref in enumerate((basis_0_ref, basis_1_ref, base_ref))]
    others += [copies.start(side_ref.at[part], images.at[part, :R]) for part in range(2)]
    far = far_part(place_ref, ranks_ref, own_ref, partner_ref, rows_copy, rows, tiles, left)
    wait(others)
    basis[2] = basis[2] + far
    sent = [copies.start(basis.at[2], basis_2_ref)]
    for j in range(2):
        for part in range(2):
            images[part, R * (j + 1) : R * (j + 2)] = basis[j + 1, part] + SHIFT * basis[j, part]
    total = [dot(images[part, R:], images[part, : 2 * R], (1, 1)) for part in range(2)]
    total = total[0] + total[1]
    last = [dot(images[part, 2 * R :], images[part, 2 * R :], (1, 1)) for part in range(2)]
    sums[: 2 * R] = total[:, :R]
    sums[2 * R : 4 * R] = total[:, R:]
    sums[4 * R :] = last[0] + last[1]
    z, core = place_ref[0], place_ref[1]
    size = mine_ref.shape[1]
    for d, ref in enumerate((mine_ref, other_ref)):
        for k in range(4):
            ref[k] = sums[aligned(4 * (core ^ d) + (z ^ k), size)]
    wait(sent)


def finish_kernel(
    place_ref, own_ref, partner_ref, side_ref, basis_0_ref, basis_1_ref, basis_2_ref, solution_ref, residual_ref,
    sums, halves, work, cross, basis, side, solved, left_over, sems,
):
    copies = Copies(sems)
    z, core = place_ref[0], place_ref[1]
    size = own_ref.shape[1]
    for d, ref in enumerate((own_ref, partner_ref)):
        for k in range(4):
            sums[aligned(4 * (core ^ d) + (z ^ k), size)] = ref[k]
    others = [copies.start(side_ref, side)]
    for i, ref in enumerate((basis_0_ref, basis_1_ref, basis_2_ref)):
        others += [copies.start(ref.at[part], basis.at[part, R * i : R * (i + 1)]) for part in range(2)]
    b_0, b_1, a_00, a_10, a_11 = (sums.at[R * i : R * (i + 1)] for i in range(5))
    work[...] = a_00[...]

    def factor(i, carry):
        halves[i] = inverse_factor(work[...])

        @pl.when(i == 0)
        def _():
            cross[...] = dot(halves[0], a_10[...], (1, 1))
            work[...] = a_11[...] - dot(cross[...], cross[...], (0, 0))

        return carry

    lax.fori_loop(0, 2, factor, 0)
    reduced = dot(halves[0], b_0[...])
    tail = dot(halves[1], b_1[...] - dot(cross[...], reduced, (0, 0)))
    y_1 = dot(tail, halves[1], (0, 0))
    y_0 = dot(reduced - dot(cross[...], y_1, (1, 1)), halves[0], (0, 0))
    weights = jnp.concatenate([y_0, y_1], axis=1)
    wait(others)
    sent = []
    for part in range(2):
        solved[part] = dot(weights, basis[part, : 2 * R])
        sent.append(copies.start(solved.at[part], solution_ref.at[part]))
        left_over[part] = side[part] - SHIFT * solved[part] - dot(weights, basis[part, R:])
        sent.append(copies.start(left_over.at[part], residual_ref.at[part]))
    wait(sent)


def swap(x, axis, k):
    n = lax.axis_size(axis)
    return lax.ppermute(x, axis, [(i, i ^ k) for i in range(n)])


def sum_axis(x, axis):
    one, two, three = (swap(x, axis, k) for k in (1, 2, 3))
    return (x + one) + (two + three)


def sum_halves(mine, other):
    total = mine + swap(other, "c", 1)
    for axis in ("z", "y", "x"):
        total = sum_axis(total, axis)
    return total, swap(total, "c", 1)


def gather_z(piece):
    own = jnp.stack([piece] + [swap(piece, "z", k) for k in (1, 2, 3)])
    return own, swap(own, "c", 1)


def sum_pieces(mine, other):
    pair = mine + swap(other, "c", 1)
    one, two, three = (swap(pair[k], "z", k) for k in (1, 2, 3))
    total = (pair[0] + one) + (two + three)
    for axis in ("y", "x"):
        total = sum_axis(total, axis)
    return gather_z(total)


def gather_coeffs(products):
    parts = lax.all_to_all(products.reshape(8 * TILES, 16, 2 * K), ALL, 0, 0, tiled=True)
    parts = parts.reshape(TILES, 8, 16, 2 * K)
    return gather_z(jnp.sum(parts.astype(jnp.float32), axis=1).astype(jnp.bfloat16))


def local(right_side, self_impedance, near_blocks, near_columns, column_factors, row_factors, tile_ranks):
    width = right_side.shape[2]
    sub_blocks = near_columns.shape[1]
    x, y, z, core = (lax.axis_index(axis) for axis in ALL)
    place = jnp.stack([z, core, 4 * x + y]).astype(jnp.int32)
    where = near_columns[0] - (2 * z + core) * sub_blocks + HALO
    columns = column_factors[0].reshape(TILES * 2 * K, width)
    rows = row_factors[0].reshape(TILES * 2 * K, width)
    near = near_blocks[0]
    forward = [(i, i + 1) for i in range(7)]
    backward = [(i + 1, i) for i in range(7)]

    def shape(*dims, dtype=jnp.float32):
        return jax.ShapeDtypeStruct(dims, dtype)

    block = shape(2, R, width)
    rounded_block = shape(2, R, width, dtype=jnp.bfloat16)
    edge = shape(2, R, HALO * SB, dtype=jnp.bfloat16)
    products_block = shape(TILES, R, 2 * K, dtype=jnp.bfloat16)
    wide = VMEM((2, R, width), jnp.float32)
    rounded_scratch = VMEM((2, R, width), jnp.bfloat16)
    products_scratch = VMEM((TILES, R, 2 * K), jnp.bfloat16)
    weights = VMEM((TILES * 2 * K, width), jnp.bfloat16)
    far_scratch = [products_scratch, VMEM((2 * R, TILES * 2 * K), jnp.bfloat16), weights]
    square = VMEM((R, R), jnp.float32)
    outer = VMEM((5 * R, R), jnp.float32)
    stacked = VMEM((2, 3 * R, width), jnp.float32)

    def call(kernel, out_specs, smem, vmem, scratch, copies, *args, limit=LARGE):
        if copies:
            scratch = [*scratch, pltpu.SemaphoreType.DMA((copies,))]
        return pl.pallas_call(
            kernel,
            out_shape=tuple(kind for kind, _ in out_specs),
            in_specs=[SMEM] * smem + [WHOLE] * vmem + [ANY] * (len(args) - smem - vmem),
            out_specs=tuple(space for _, space in out_specs),
            scratch_shapes=scratch,
            compiler_params=pltpu.CompilerParams(vmem_limit_bytes=limit),
            cost_estimate=pl.CostEstimate(flops=3 * 10**8, bytes_accessed=6 * 2**20, transcendentals=0),
        )(*args)

    def operate(x, rounded, low, high, products):
        from_right = lax.ppermute(low, ("z", "c"), backward)
        from_left = lax.ppermute(high, ("z", "c"), forward)
        own, partner = gather_coeffs(products)
        (base,) = call(
            near_kernel,
            ((block, ANY),),
            1,
            0,
            [
                wide,
                VMEM((2, R, width + 2 * HALO * SB), jnp.bfloat16),
                VMEM((2, width), jnp.float32),
                VMEM(near.shape, jnp.bfloat16),
                VMEM((2 * R, SLOTS * SB), jnp.bfloat16),
                wide,
            ],
            7,
            where, x, rounded, from_left, from_right, self_impedance, near,
        )
        return own, partner, base

    half = (shape(R // 2, R), WHOLE)
    gram = call(gram_kernel, (half, half), 1, 1, [square], 0, place, right_side, limit=SMALL)
    operands = ((block, ANY), (rounded_block, ANY), (edge, ANY), (edge, ANY), (products_block, ANY))
    basis_0, *rest = call(
        start_kernel, operands, 1, 2, [square, wide, weights, wide, rounded_scratch, products_scratch], 10,
        place, *sum_halves(*gram), right_side, columns,
    )
    own, partner, base = operate(basis_0, *rest)
    basis_1, *rest = call(
        middle_kernel, operands, 2, 2, [*far_scratch, weights, wide, rounded_scratch, products_scratch], 11,
        place, tile_ranks, own, partner, rows, base, columns,
    )
    own, partner, base = operate(basis_1, *rest)
    pieces = (shape(4, 5 * R // 8, R), WHOLE)
    basis_2, *sums = call(
        last_kernel, ((block, ANY), pieces, pieces), 2, 2,
        [*far_scratch, VMEM((3, 2, R, width), jnp.float32), stacked, outer], 7,
        place, tile_ranks, own, partner, rows, base, right_side, basis_0, basis_1,
    )
    return call(
        finish_kernel, ((block, ANY), (block, ANY)), 1, 2,
        [outer, VMEM((2, R, R), jnp.float32), square, square, stacked, wide, wide, wide], 11,
        place, *sum_pieces(*sums), right_side, basis_0, basis_1, basis_2,
    )


def solution(mesh):
    fine = Mesh(mesh.devices.reshape(4, 4, 4, 2), ALL)
    row, col = ("x", "y"), ("z", "c")
    placed = (
        P(None, None, ALL),
        P(None, ALL),
        P(row, col, None, None, None, None),
        P(row, col, None),
        P(row, None, None, None, col),
        P(row, None, None, None, col),
        P(),
    )
    return jax.shard_map(
        local, mesh=fine, in_specs=placed, out_specs=(P(None, None, ALL), P(None, None, ALL)), check_vma=False
    )
```
